32 devices in a mesh: dom: 8 (over y, x, core), seq: 4 (over z).
Axes of the slice: x: 2, y: 2, z: 4, core: 2. Of those that a mesh axis runs over, the one named last changes fastest.
Arguments:
- hidden: bfloat16 [8, 160, 3072], P('dom', 'seq'), may hold values from -6 to 6
- qkv: bfloat16 [8, 160, 12288], P('dom', 'seq'), may hold values from -10 to 10
- w_out: bfloat16 [4096, 3072], P('seq'), may hold values from -0.09375 to 0.09375
- gate: float32 [3072], replicated, may hold values from 2 to 6
- next_scale: float32 [3072], replicated, may hold values from -0.5 to 1.5
- ancestors: int32 [8], replicated, may hold values from 0 to 7, as said below
- w_next: bfloat16 [3072, 12288], P('dom', 'seq'), may hold values from -0.109375 to 0.109375
Outputs:
- next_hidden: bfloat16 [8, 160, 3072], P('dom', 'seq')
- next_qkv: bfloat16 [8, 160, 12288], P('dom', None, 'seq')
The draws below stay inside these ranges and needn't reach their ends.
Inputs may be any that keep to these rules, and one draw needn't show every extreme that they name: `ancestors`: at least one particle p continues particle p - 1, and at least one particle p continues particle p + 8 // 2 (both counted round).
All inputs are finite; a program needn't handle non-finite values.
Results may differ from the reference program's by a relative error of at most 0.017.
Values may be sent and summed in bfloat16 or wider, within the bound.
A program may use at most 64 MiB of HBM per device.

```python
import jax
import jax.numpy as jnp
from jax import lax

D = 3072
HEAD_DIM = 128
HEADS = 32
PARTICLES = 8
SEQ = 160
HD = 4096
N_SEQ = 4


def draw_qkv(key, part):
    shape = (PARTICLES, SEQ, HEADS, 3, HEAD_DIM)
    base = jnp.clip(jax.random.normal(key, shape, jnp.float32), -4.0, 4.0)
    return base.reshape(PARTICLES, SEQ, HEADS * 3 * HEAD_DIM).astype(jnp.bfloat16)


def draw_ancestors(key, part):
    first_key = jax.random.fold_in(key, 11)
    second_key = jax.random.fold_in(key, 23)
    label_key = jax.random.fold_in(key, 37)
    chosen_key = jax.random.fold_in(key, 41)
    first = jax.random.randint(first_key, (PARTICLES,), 0, PARTICLES, dtype=jnp.int32)
    second = jax.random.randint(second_key, (PARTICLES,), 0, PARTICLES, dtype=jnp.int32)
    ranked = jnp.minimum(first, second)
    labels = jax.random.permutation(label_key, PARTICLES).astype(jnp.int32)
    base = jnp.take(labels, ranked, axis=0).astype(jnp.int32)
    chosen = jax.random.randint(chosen_key, (), 0, PARTICLES, dtype=jnp.int32)
    before = ((chosen + PARTICLES - 1) % PARTICLES).astype(jnp.int32)
    opposite = ((chosen + PARTICLES // 2) % PARTICLES).astype(jnp.int32)
    positions = jnp.arange(PARTICLES, dtype=jnp.int32)
    result = jnp.where(positions == chosen, before, base).astype(jnp.int32)
    return jnp.where(positions == opposite, chosen, result).astype(jnp.int32)


def levels(own_key, shape, cuts, low, top_value):
    gain = 1.0
    for position, shards_of in cuts:
        heights = jax.random.uniform(jax.random.fold_in(jax.random.fold_in(own_key, 6), position), (shards_of,), jnp.float32, low / len(cuts), top_value / len(cuts))
        gain = gain * jnp.repeat(jnp.exp(heights), shape[position] // shards_of).reshape((-1,) + (1,) * (len(shape) - 1 - position))
    return gain


def gaussian(rng, dims, spread, most, cuts=(), kind=jnp.bfloat16):
    factor_of = levels(rng, dims, cuts, -0.22, 0.18) if cuts else 1.0
    drawn = jax.random.normal(rng, dims, jnp.float32) * spread * factor_of
    return jnp.minimum(jnp.maximum(drawn, -most), most).astype(kind)


def setup_inputs(seed: int = 0) -> dict:
    key_of = jax.random.split(jax.random.key(seed), 8)
    return {
        "hidden": gaussian(key_of[0], (PARTICLES, SEQ, D), 1.0, 6.0, ((0, 8), (1, 4))),
        "qkv": draw_qkv(jax.random.fold_in(key_of[7], 71), 0),
        "w_out": gaussian(key_of[2], (HD, D), HD ** -0.5, 0.09375, ((0, 4),)),
        "gate": jnp.clip(jax.random.uniform(key_of[3], (D,), jnp.float32, 2.0, 6.0), 2.0, 6.0),
        "next_scale": jnp.clip(jax.random.uniform(key_of[4], (D,), jnp.float32, -0.5, 1.5), -0.5, 1.5),
        "ancestors": draw_ancestors(jax.random.fold_in(key_of[7], 71), 0),
        "w_next": gaussian(key_of[6], (D, 3 * HD), D ** -0.5, 0.109375, ((0, 8), (1, 4))),
    }


def attend(block):
    layout = block.reshape(SEQ, HEADS, 3, HEAD_DIM).astype(jnp.float32)
    scores = jnp.einsum('qhd,khd->hqk', layout[:, :, 0], layout[:, :, 1]) * HEAD_DIM ** (-0.5)
    attn_weights = jax.nn.softmax(scores, axis=-1).astype(jnp.bfloat16)
    attn_weights = lax.optimization_barrier(attn_weights).astype(jnp.float32)
    attended = jnp.einsum('hqk,khd->qhd', attn_weights, layout[:, :, 2])
    return attended.astype(jnp.bfloat16).reshape(SEQ, HEADS * HEAD_DIM)

def block_update(hidden_rows, qkv_rows, w_out, gate):
    attended = attend(qkv_rows)
    group_cols = HEADS * HEAD_DIM // N_SEQ
    grouped = attended.reshape(SEQ, N_SEQ, group_cols).astype(jnp.float32)
    w_groups = w_out.reshape(N_SEQ, group_cols, D).astype(jnp.float32)
    partial_terms = jnp.einsum('sgc,gcd->gsd', grouped, w_groups)
    partial_terms = lax.optimization_barrier(partial_terms.astype(jnp.bfloat16)).astype(jnp.float32)
    branch = lax.optimization_barrier(jnp.sum(partial_terms, axis=0))
    return (hidden_rows.astype(jnp.float32) + gate * branch).astype(jnp.bfloat16)

def reference(hidden, qkv, w_out, gate, next_scale, ancestors, w_next):
    updated = lax.map(lambda both_rows: block_update(both_rows[0], both_rows[1], w_out, gate), (hidden, qkv))
    next_hidden = jnp.take(updated, ancestors.astype(jnp.int32), axis=0)
    widened = next_hidden.astype(jnp.float32)
    squares = lax.optimization_barrier(jnp.mean(widened * widened, axis=-1, keepdims=True))
    normed = (widened * lax.rsqrt(squares + 1e-06) * (1.0 + next_scale)).astype(jnp.bfloat16)
    next_qkv = lax.map(lambda normed_rows: jnp.dot(normed_rows, w_next, preferred_element_type=jnp.float32).astype(jnp.bfloat16), normed)
    return (next_hidden, next_qkv)
```

```python
import functools

import jax
import jax.numpy as jnp
from jax import lax
from jax.experimental import pallas as pl
from jax.experimental.pallas import tpu as pltpu
from jax.sharding import PartitionSpec as P

HEAD_DIM = 128
MESH = pl.DeviceIdType.MESH
F32 = jnp.float32
BF16 = jnp.bfloat16
UNIT = 8
CHUNKS = 5
HEAD_GROUPS = 4


def tile_of(width, most):
    return max(t for t in range(128, most + 1, 128) if width % t == 0)


def grid_of(dom_n):
    chips = dom_n // 2
    cx = max(c for c in range(1, chips + 1) if chips % c == 0 and c * c <= chips)
    return chips // cx, cx


def unit_of(rows):
    return UNIT if rows % UNIT == 0 else rows


def chunks_of(units):
    n = min(CHUNKS, units)
    edges = [units * i // n for i in range(n + 1)]
    return list(zip(edges[:-1], edges[1:]))


def groups_of(heads):
    n = max(g for g in range(1, HEAD_GROUPS + 1) if heads % g == 0)
    return [(heads // n * g, heads // n) for g in range(n)]


def kernel(dom_n, seq_n, chunks, *refs):
    n_c = len(chunks)
    (anc_ref, hidden_ref, qkv_ref, wout_ref, gate_ref, scale_ref, wnext_ref, nh_ref, out_ref,
     heads, wout_v, hid_v, att, part, rs_in, pieces_n, pieces_h) = refs[:17]
    arrived = refs[17:17 + n_c]
    (arrived_h, routed_h, landed, z_all, lhs_a, lhs_b, act_a, act_b, w_a, w_b, acc, snd_a, snd_b, rcv_a, rcv_b,
     loc_sem, q_s, q_r, rs_s, rs_r, n_s, n_r, z_s, z_r, la_s, la_r, lb_s, lb_r, oa_s, oa_r, ob_s, ob_r,
     h_s, h_r, b_s, b_r, wa_s, wa_r, wb_s, wb_r, ma_s, ma_r, mb_s, mb_r, own_sem) = refs[17 + n_c:]

    cy, cx = grid_of(dom_n)
    d = lax.axis_index("dom")
    s = lax.axis_index("seq")
    core = lax.rem(d, 2)
    chip = d // 2
    col = lax.rem(chip, cx)
    row = chip // cx
    mate = d + 1 - 2 * core
    units, unit, width = hid_v.shape
    seq_len = seq_n * units * unit
    cols = heads.shape[2]
    head_n = cols // (3 * HEAD_DIM)
    groups = groups_of(head_n)
    gcols = groups[0][1] * 3 * HEAD_DIM
    wrows = wnext_ref.shape[0]
    wcols = w_a.shape[1]
    piece = width // dom_n

    def dev(r, c, k):
        return ((r * cx + c) * 2 + k, s)

    def push(src, dst, send, recv, to):
        return pltpu.make_async_remote_copy(
            src_ref=src, dst_ref=dst, send_sem=send, recv_sem=recv, device_id=to, device_id_type=MESH
        )

    def keep(src, dst, sem):
        c = pltpu.make_async_copy(src, dst, sem)
        c.start()
        return c

    def wslot(ref, slot):
        return ref.at[pl.ds(pl.multiple_of(slot * wrows, 16), wrows), :]

    slot_a = row * 2 + core
    slot_b = col * 2 + core
    src_a = wnext_ref.at[:, pl.ds(0, wcols)]
    src_b = wnext_ref.at[:, pl.ds(wcols, wcols)]

    def head_src(to, g):
        return qkv_ref.at[0, :, pl.ds(pl.multiple_of(to * cols + g * gcols, 128), gcols)]

    own_heads = [
        keep(head_src(s, g), heads.at[s, :, pl.ds(g * gcols, gcols)], loc_sem.at[4 + g])
        for g in range(len(groups))
    ]
    wout_copy = keep(wout_ref, wout_v, loc_sem.at[0])
    hid_copy = keep(hidden_ref, hid_v, loc_sem.at[1])
    own_a = keep(src_a, wslot(w_a, slot_a), loc_sem.at[2])
    own_b = keep(src_b, wslot(w_b, slot_b), loc_sem.at[3])

    barrier = pltpu.get_barrier_semaphore()
    for k in range(1, seq_n):
        pl.semaphore_signal(barrier, inc=1, device_id=(d, lax.rem(s + k, seq_n)), device_id_type=MESH)
    for k in range(1, dom_n):
        pl.semaphore_signal(barrier, inc=1, device_id=(lax.rem(d + k, dom_n), s), device_id_type=MESH)
    pl.semaphore_wait(barrier, seq_n - 1 + dom_n - 1)

    sent = []

    def start(c):
        c.start()
        sent.append(c)
        return c

    order = sorted(range(1, seq_n), key=lambda k: -min(k, seq_n - k))
    q_copies = []
    for g in range(len(groups)):
        q_copies.append([
            start(push(
                head_src(lax.rem(s + k, seq_n), g), heads.at[s, :, pl.ds(g * gcols, gcols)],
                q_s.at[g, k], q_r.at[g, k], (d, lax.rem(s + k, seq_n)),
            ))
            for k in order
        ])

    wa_copies = [
        start(push(src_a, wslot(w_a, slot_a), wa_s.at[q], wa_r.at[q], dev(lax.rem(row + q, cy), col, core)))
        for q in range(1, cy)
    ]
    wb_copies = [
        start(push(src_b, wslot(w_b, slot_b), wb_s.at[q], wb_r.at[q], dev(row, lax.rem(col + q, cx), core)))
        for q in range(1, cx)
    ]
    mate_copies = [
        start(push(src_a, wslot(w_a, slot_a), ma_s.at[0], ma_r.at[0], (mate, s))),
        start(push(src_b, wslot(w_b, slot_b), mb_s.at[0], mb_r.at[0], (mate, s))),
    ]

    def forward_weights():
        for q in range(1, cy):
            wa_copies[q - 1].wait_recv()
            slot = wslot(w_a, lax.rem(row + cy - q, cy) * 2 + core)
            mate_copies.append(start(push(slot, slot, ma_s.at[q], ma_r.at[q], (mate, s))))
        for q in range(1, cx):
            wb_copies[q - 1].wait_recv()
            slot = wslot(w_b, lax.rem(col + cx - q, cx) * 2 + core)
            mate_copies.append(start(push(slot, slot, mb_s.at[q], mb_r.at[q], (mate, s))))

    def merge(x):
        return x.astype(F32).reshape(seq_len, x.shape[-1]).astype(BF16)

    def unit_major(x):
        x = x.astype(F32).reshape(seq_n, units, unit, x.shape[-1])
        return jnp.transpose(x, (1, 0, 2, 3)).reshape(seq_len, x.shape[-1]).astype(BF16)

    def one_head(h, carry):
        base = pl.multiple_of(h * 3 * HEAD_DIM, HEAD_DIM)
        q = unit_major(heads[:, :, pl.ds(base, HEAD_DIM)])
        key = merge(heads[:, :, pl.ds(pl.multiple_of(base + HEAD_DIM, HEAD_DIM), HEAD_DIM)])
        v = merge(heads[:, :, pl.ds(pl.multiple_of(base + 2 * HEAD_DIM, HEAD_DIM), HEAD_DIM)])
        sc = lax.dot_general(q, key, (((1,), (1,)), ((), ())), preferred_element_type=F32)
        sc = sc * HEAD_DIM ** (-0.5)
        e = jnp.exp(sc - jnp.max(sc, axis=-1, keepdims=True))
        w = (e / jnp.sum(e, axis=-1, keepdims=True)).astype(BF16)
        o = jnp.dot(w, v, preferred_element_type=F32).astype(BF16)
        att[:, pl.ds(pl.multiple_of(h * HEAD_DIM, HEAD_DIM), HEAD_DIM)] = o
        return carry

    for g, (first, count) in enumerate(groups):
        own_heads[g].wait()
        for c in q_copies[g]:
            c.wait_recv()
        lax.fori_loop(first, first + count, one_head, 0)
    wout_copy.wait()

    tile = tile_of(width, 512)
    wide = tile_of(wcols, 512)
    state = {}

    def project(c):
        u0, u1 = chunks[c]
        n = u1 - u0
        m = seq_n * unit

        def step(t, carry):
            c0 = pl.ds(pl.multiple_of(t * tile, 128), tile)
            y = jnp.dot(att[u0 * m:u1 * m, :], wout_v[:, c0], preferred_element_type=F32)
            y = y.reshape(n, seq_n, unit, tile).astype(BF16)
            for u in range(n):
                part[:, u0 + u, :, c0] = y[u]
            return carry

        lax.fori_loop(0, width // tile, step, 0)
        state["rs", c] = [
            start(push(
                part.at[lax.rem(s + k, seq_n), pl.ds(u0, n)], rs_in.at[s, pl.ds(u0, n)],
                rs_s.at[c, k], rs_r.at[c, k], (d, lax.rem(s + k, seq_n)),
            ))
            for k in order
        ]

    def update(c):
        u0, u1 = chunks[c]
        if c == 0:
            hid_copy.wait()
        for cp in state["rs", c]:
            cp.wait_recv()
        for u in range(u0, u1):
            kept = []
            squares = jnp.zeros((unit, piece), F32)
            for j in range(dom_n):
                c0 = slice(j * piece, (j + 1) * piece)
                total = part[s, u, :, c0].astype(F32)
                for k in range(1, seq_n):
                    total = total + rs_in[lax.rem(s + k, seq_n), u, :, c0].astype(F32)
                x = (hid_v[u, :, c0].astype(F32) + gate_ref[:, c0] * total).astype(BF16)
                pieces_h[j, u] = x
                x = x.astype(F32)
                squares = squares + x * x
                kept.append(x)
            inv = lax.rsqrt(jnp.sum(squares, axis=-1, keepdims=True) / width + 1e-06)
            for j in range(dom_n):
                c0 = slice(j * piece, (j + 1) * piece)
                pieces_n[j, u] = (kept[j] * inv * (1.0 + scale_ref[:, c0])).astype(BF16)
        state["n", c] = [
            start(push(
                pieces_n.at[lax.rem(d + k, dom_n), pl.ds(u0, u1 - u0)], arrived[c].at[d],
                n_s.at[c, k], n_r.at[c, k], (lax.rem(d + k, dom_n), s),
            ))
            for k in range(1, dom_n)
        ]
        arrived[c][d] = pieces_n[d, u0:u1]
        if c == n_c - 1:
            state["h"] = [
                start(push(
                    pieces_h.at[lax.rem(d + k, dom_n)], arrived_h.at[d],
                    h_s.at[k], h_r.at[k], (lax.rem(d + k, dom_n), s),
                ))
                for k in range(1, dom_n)
            ]
            arrived_h[d] = pieces_h[d]

    def route(c):
        u0, u1 = chunks[c]
        for cp in state["n", c]:
            cp.wait_recv()
        for p in range(dom_n):
            z_all[p // 2 // cx, p // 2 % cx, p % 2, s, u0:u1] = arrived[c][anc_ref[p]]
        block = z_all.at[:, :, :, s, pl.ds(u0, u1 - u0)]
        state["z", c] = [
            start(push(block, block, z_s.at[c, k], z_r.at[c, k], (d, lax.rem(s + k, seq_n))))
            for k in order
        ]

    def route_hidden():
        for cp in state["h"]:
            cp.wait_recv()
        for p in range(dom_n):
            routed_h[p] = arrived_h[anc_ref[p]]
        state["b"] = [
            start(push(
                routed_h.at[lax.rem(d + k, dom_n)], landed.at[d],
                b_s.at[k], b_r.at[k], (lax.rem(d + k, dom_n), s),
            ))
            for k in range(1, dom_n)
        ]
        landed[d] = routed_h[d]

    def finish_hidden():
        for cp in state["b"]:
            cp.wait_recv()
        for j in range(dom_n):
            nh_ref[:, :, j * piece:(j + 1) * piece] = landed[j]

    def hand_out(c):
        u0, u1 = chunks[c]
        us = pl.ds(u0, u1 - u0)
        for cp in state["z", c]:
            cp.wait_recv()
        copies = []
        for q in range(cy):
            for kk in range(2):
                r, k = lax.rem(row + q, cy), core + kk - 2 * kk * core
                src = z_all.at[r, :, k, :, us]
                dst = lhs_a.at[slot_a, :, :, us]
                if q == 0 and kk == 0:
                    state["oa", c] = keep(src, dst, own_sem.at[c, 0])
                else:
                    i = q * 2 + kk
                    copies.append(start(push(src, dst, la_s.at[c, i], la_r.at[c, i], dev(r, col, k))))
        for q in range(cx):
            for kk in range(2):
                r, k = lax.rem(col + q, cx), core + kk - 2 * kk * core
                src = z_all.at[:, r, k, :, us]
                dst = lhs_b.at[slot_b, :, :, us]
                if q == 0 and kk == 0:
                    state["ob", c] = keep(src, dst, own_sem.at[c, 1])
                else:
                    i = q * 2 + kk
                    copies.append(start(push(src, dst, lb_s.at[c, i], lb_r.at[c, i], dev(row, r, k))))
        state["l", c] = copies

    def multiply(c):
        u0, u1 = chunks[c]
        n = u1 - u0
        m = seq_n * n * unit
        if c == 0:
            own_a.wait()
            own_b.wait()
            for cp in mate_copies:
                cp.wait_recv()
        state["oa", c].wait()
        state["ob", c].wait()
        for cp in state["l", c]:
            cp.wait_recv()
        state["o", c] = []
        for half, (lhs, act, w, snd, rcv, ss, rr, here, many) in enumerate((
            (lhs_a, act_a, w_a, snd_a, rcv_a, oa_s, oa_r, col, cx),
            (lhs_b, act_b, w_b, snd_b, rcv_b, ob_s, ob_r, row, cy),
        )):
            for q in range(many):
                for j in range(lhs.shape[0]):
                    x = lhs[j, lax.rem(here + q, many), :, u0:u1].astype(F32)
                    act[q * m:(q + 1) * m, j * piece:(j + 1) * piece] = x.reshape(m, piece).astype(BF16)

            def step(t, carry, half=half, act=act, w=w, snd=snd, many=many):
                c0 = pl.ds(pl.multiple_of(t * wide, 128), wide)
                o0 = pl.ds(pl.multiple_of(half * wcols + t * wide, 128), wide)
                y = jnp.dot(act[:many * m, :], w[:, c0], preferred_element_type=F32)
                y = y.reshape(many, seq_n, n, unit, wide)
                acc[:, u0:u1, :, o0] = y[0]
                for q in range(1, many):
                    snd[q - 1, :, u0:u1, :, c0] = y[q].astype(BF16)
                return carry

            lax.fori_loop(0, wcols // wide, step, 0)
            for q in range(1, many):
                to = lax.rem(here + q, many)
                state["o", c].append(start(push(
                    snd.at[q - 1, :, pl.ds(u0, n)], rcv.at[q - 1, :, pl.ds(u0, n)],
                    ss.at[c, q], rr.at[c, q],
                    dev(row, to, core) if half == 0 else dev(to, col, core),
                )))

    def finish(c):
        u0, u1 = chunks[c]
        for cp in state["o", c]:
            cp.wait_recv()
        for half, (rcv, many) in enumerate(((rcv_a, cx), (rcv_b, cy))):
            def step(t, carry, half=half, rcv=rcv, many=many):
                c0 = pl.ds(pl.multiple_of(t * wide, 128), wide)
                o0 = pl.ds(pl.multiple_of(half * wcols + t * wide, 128), wide)
                y = acc[:, u0:u1, :, o0]
                for q in range(1, many):
                    y = y + rcv[q - 1, :, u0:u1, :, c0].astype(F32)
                out_ref[:, u0:u1, :, o0] = y.astype(BF16)
                return carry

            lax.fori_loop(0, wcols // wide, step, 0)

    stages = (project, update, route, hand_out, multiply, finish)
    for t in range(n_c + len(stages) - 1):
        for i, stage in enumerate(stages):
            if 0 <= t - i < n_c:
                stage(t - i)
        if t == 1:
            forward_weights()
        if t == n_c + 1:
            route_hidden()
        if t == n_c + 3:
            finish_hidden()
    for c in sent:
        c.wait_send()


def body(dom_n, seq_n, hidden, qkv, w_out, gate, next_scale, ancestors, w_next):
    _, rows, width = hidden.shape
    unit = unit_of(rows)
    units = rows // unit
    chunks = chunks_of(units)
    n_c = len(chunks)
    cols = qkv.shape[2] // seq_n
    seq_len = rows * seq_n
    out_cols = w_next.shape[1]
    wcols = out_cols // 2
    att_cols = w_out.shape[0]
    cy, cx = grid_of(dom_n)
    piece = width // dom_n
    n_g = len(groups_of(cols // (3 * HEAD_DIM)))
    most = max(u1 - u0 for u0, u1 in chunks) * seq_n * unit
    sem = pltpu.SemaphoreType.DMA
    any_spec = pl.BlockSpec(memory_space=pl.ANY)
    vmem = pl.BlockSpec(memory_space=pltpu.VMEM)

    def buf(*shape, dtype=BF16):
        return pltpu.VMEM(shape, dtype)

    nh, out = pl.pallas_call(
        functools.partial(kernel, dom_n, seq_n, chunks),
        out_shape=(
            jax.ShapeDtypeStruct((units, unit, width), BF16),
            jax.ShapeDtypeStruct((seq_n, units, unit, out_cols), BF16),
        ),
        in_specs=[
            pl.BlockSpec(memory_space=pltpu.SMEM), any_spec, any_spec, any_spec, vmem, vmem, any_spec,
        ],
        out_specs=(vmem, vmem),
        scratch_shapes=[
            buf(seq_n, rows, cols),
            buf(att_cols, width),
            buf(units, unit, width),
            buf(seq_len, att_cols),
            buf(seq_n, units, unit, width),
            buf(seq_n, units, unit, width),
            buf(dom_n, units, unit, piece),
            buf(dom_n, units, unit, piece),
            *[buf(dom_n, u1 - u0, unit, piece) for u0, u1 in chunks],
            buf(dom_n, units, unit, piece),
            buf(dom_n, units, unit, piece),
            buf(dom_n, units, unit, piece),
            buf(cy, cx, 2, seq_n, units, unit, piece),
            buf(2 * cy, cx, seq_n, units, unit, piece),
            buf(2 * cx, cy, seq_n, units, unit, piece),
            buf(cx * most, 2 * cy * piece),
            buf(cy * most, 2 * cx * piece),
            buf(2 * cy * w_next.shape[0], wcols),
            buf(2 * cx * w_next.shape[0], wcols),
            buf(seq_n, units, unit, out_cols, dtype=F32),
            buf(max(cx - 1, 1), seq_n, units, unit, wcols),
            buf(max(cy - 1, 1), seq_n, units, unit, wcols),
            buf(max(cx - 1, 1), seq_n, units, unit, wcols),
            buf(max(cy - 1, 1), seq_n, units, unit, wcols),
            sem((4 + n_g,)),
            sem((n_g, seq_n)), sem((n_g, seq_n)),
            sem((n_c, seq_n)), sem((n_c, seq_n)),
            sem((n_c, dom_n)), sem((n_c, dom_n)),
            sem((n_c, seq_n)), sem((n_c, seq_n)),
            sem((n_c, 2 * cy)), sem((n_c, 2 * cy)),
            sem((n_c, 2 * cx)), sem((n_c, 2 * cx)),
            sem((n_c, cx)), sem((n_c, cx)),
            sem((n_c, cy)), sem((n_c, cy)),
            sem((dom_n,)), sem((dom_n,)),
            sem((dom_n,)), sem((dom_n,)),
            sem((cy,)), sem((cy,)),
            sem((cx,)), sem((cx,)),
            sem((cy,)), sem((cy,)),
            sem((cx,)), sem((cx,)),
            sem((n_c, 2)),
        ],
        compiler_params=pltpu.CompilerParams(
            collective_id=0, has_side_effects=True, vmem_limit_bytes=60 * 1024 * 1024
        ),
    )(
        ancestors, hidden.reshape(units, unit, width), qkv, w_out, gate[None], next_scale[None], w_next
    )
    return nh.reshape(1, rows, width), out.reshape(1, seq_len, out_cols)


def solution(mesh):
    in_specs = (
        P("dom", "seq", None),
        P("dom", "seq", None),
        P("seq", None),
        P(),
        P(),
        P(),
        P("dom", "seq"),
    )
    out_specs = (P("dom", "seq", None), P("dom", None, "seq"))
    return jax.shard_map(
        functools.partial(body, mesh.shape["dom"], mesh.shape["seq"]),
        mesh=mesh, in_specs=in_specs, out_specs=out_specs, check_vma=False,
    )
```

```python
import functools

import jax
import jax.numpy as jnp
from jax import lax
from jax.experimental import pallas as pl
from jax.experimental.pallas import tpu as pltpu
from jax.sharding import PartitionSpec as P

HEAD_DIM = 128
MESH = pl.DeviceIdType.MESH
F32 = jnp.float32
BF16 = jnp.bfloat16
UNIT = 8
SPLIT = (1, 2, 2)
BATCHES = (1, 1, 1)
OFFSETS = (0, 1, 2, 3, 4, 5, 6)
AHEAD = 1
FORWARD = 1
WEIGHTS = -1
HEAD_GROUPS = 2


def tile_of(width, most):
    return max(t for t in range(128, most + 1, 128) if width % t == 0)


def grid_of(dom_n):
    chips = dom_n // 2
    cx = max(c for c in range(1, chips + 1) if chips % c == 0 and c * c <= chips)
    return chips // cx, cx


def unit_of(rows):
    return UNIT if rows % UNIT == 0 else rows


def chunks_of(units):
    edges = [0]
    for n in SPLIT:
        edges.append(edges[-1] + n)
    cuts = sorted({units * e // edges[-1] for e in edges})
    return list(zip(cuts[:-1], cuts[1:]))


def batches_of(n_c):
    edges = [0]
    for n in BATCHES:
        edges.append(min(edges[-1] + n, n_c))
    edges[-1] = n_c
    cuts = sorted(set(edges))
    return list(zip(cuts[:-1], cuts[1:]))


def groups_of(heads):
    n = max(g for g in range(1, HEAD_GROUPS + 1) if heads % g == 0)
    return [(heads // n * g, heads // n) for g in range(n)]


def kernel(dom_n, seq_n, chunks, *refs):
    n_c = len(chunks)
    (anc_ref, hidden_ref, qkv_ref, wout_ref, gate_ref, scale_ref, wnext_ref, nh_ref, out_ref,
     heads, wout_v, hid_v, att, part, rs_in, rs_x, fwd, pieces_n, pieces_h) = refs[:19]
    arrived = refs[19:19 + n_c]
    (arrived_h, routed_h, landed, z_all, lhs_a, lhs_b, act_a, act_b, w_a, w_b, acc, snd_a, snd_b, rcv_a, rcv_b,
     loc_sem, q_s, q_r, rs_s, rs_r, x_s, x_r, n_s, n_r, z_s, z_r, la_s, la_r, lb_s, lb_r, oa_s, oa_r, ob_s, ob_r,
     h_s, h_r, b_s, b_r, wa_s, wa_r, wb_s, wb_r, ma_s, ma_r, mb_s, mb_r, own_sem) = refs[19 + n_c:]

    cy, cx = grid_of(dom_n)
    d = lax.axis_index("dom")
    s = lax.axis_index("seq")
    core = lax.rem(d, 2)
    chip = d // 2
    col = lax.rem(chip, cx)
    row = chip // cx
    mate = d + 1 - 2 * core
    units, unit, width = hid_v.shape
    seq_len = seq_n * units * unit
    cols = heads.shape[2]
    head_n = cols // (3 * HEAD_DIM)
    groups = groups_of(head_n)
    gcols = groups[0][1] * 3 * HEAD_DIM
    wrows = wnext_ref.shape[0]
    wcols = w_a.shape[1]
    piece = width // dom_n

    def dev(r, c, k):
        return ((r * cx + c) * 2 + k, s)

    def push(src, dst, send, recv, to):
        return pltpu.make_async_remote_copy(
            src_ref=src, dst_ref=dst, send_sem=send, recv_sem=recv, device_id=to, device_id_type=MESH
        )

    def keep(src, dst, sem):
        c = pltpu.make_async_copy(src, dst, sem)
        c.start()
        return c

    def wslot(ref, slot):
        return ref.at[pl.ds(pl.multiple_of(slot * wrows, 16), wrows), :]

    slot_a = row * 2 + core
    slot_b = col * 2 + core
    src_a = wnext_ref.at[:, pl.ds(0, wcols)]
    src_b = wnext_ref.at[:, pl.ds(wcols, wcols)]

    def head_src(to, g):
        return qkv_ref.at[0, :, pl.ds(pl.multiple_of(to * cols + g * gcols, 128), gcols)]

    own_heads = [
        keep(head_src(s, g), heads.at[s, :, pl.ds(g * gcols, gcols)], loc_sem.at[4 + g])
        for g in range(len(groups))
    ]
    wout_copy = keep(wout_ref, wout_v, loc_sem.at[0])
    hid_copy = keep(hidden_ref, hid_v, loc_sem.at[1])
    own_a = keep(src_a, wslot(w_a, slot_a), loc_sem.at[2])
    own_b = keep(src_b, wslot(w_b, slot_b), loc_sem.at[3])

    barrier = pltpu.get_barrier_semaphore()
    for k in range(1, seq_n):
        pl.semaphore_signal(barrier, inc=1, device_id=(d, lax.rem(s + k, seq_n)), device_id_type=MESH)
    for k in range(1, dom_n):
        pl.semaphore_signal(barrier, inc=1, device_id=(lax.rem(d + k, dom_n), s), device_id_type=MESH)
    pl.semaphore_wait(barrier, seq_n - 1 + dom_n - 1)

    line = seq_n == 4
    if line:
        beside = s + 1 - 2 * lax.rem(s, 2)
        mirror = 3 - s
        mirror_beside = mirror + 1 - 2 * lax.rem(mirror, 2)
        lo = 2 - 2 * (s // 2)
        middle = s * (3 - s) == 2
    sent = []
    ends_sent = []
    middle_sent = []

    def start(c):
        c.start()
        sent.append(c)
        return c

    order = sorted(range(1, seq_n), key=lambda k: -min(k, seq_n - k))
    q_copies = []
    for g in range(len(groups)):
        q_copies.append([
            start(push(
                head_src(lax.rem(s + k, seq_n), g), heads.at[s, :, pl.ds(g * gcols, gcols)],
                q_s.at[g, k], q_r.at[g, k], (d, lax.rem(s + k, seq_n)),
            ))
            for k in order
        ])

    wa_copies, wb_copies, mate_copies = [], [], []

    def spread_weights():
        wa_copies[:] = [
            start(push(src_a, wslot(w_a, slot_a), wa_s.at[q], wa_r.at[q], dev(lax.rem(row + q, cy), col, core)))
            for q in range(1, cy)
        ]
        wb_copies[:] = [
            start(push(src_b, wslot(w_b, slot_b), wb_s.at[q], wb_r.at[q], dev(row, lax.rem(col + q, cx), core)))
            for q in range(1, cx)
        ]
        mate_copies[:] = [
            start(push(src_a, wslot(w_a, slot_a), ma_s.at[0], ma_r.at[0], (mate, s))),
            start(push(src_b, wslot(w_b, slot_b), mb_s.at[0], mb_r.at[0], (mate, s))),
        ]

    def forward_weights():
        for q in range(1, cy):
            wa_copies[q - 1].wait_recv()
            slot = wslot(w_a, lax.rem(row + cy - q, cy) * 2 + core)
            mate_copies.append(start(push(slot, slot, ma_s.at[q], ma_r.at[q], (mate, s))))
        for q in range(1, cx):
            wb_copies[q - 1].wait_recv()
            slot = wslot(w_b, lax.rem(col + cx - q, cx) * 2 + core)
            mate_copies.append(start(push(slot, slot, mb_s.at[q], mb_r.at[q], (mate, s))))

    def merge(x):
        return x.astype(F32).reshape(seq_len, x.shape[-1]).astype(BF16)

    def unit_major(x):
        x = x.astype(F32).reshape(seq_n, units, unit, x.shape[-1])
        return jnp.transpose(x, (1, 0, 2, 3)).reshape(seq_len, x.shape[-1]).astype(BF16)

    def one_head(h, carry):
        base = pl.multiple_of(h * 3 * HEAD_DIM, HEAD_DIM)
        q = unit_major(heads[:, :, pl.ds(base, HEAD_DIM)])
        key = merge(heads[:, :, pl.ds(pl.multiple_of(base + HEAD_DIM, HEAD_DIM), HEAD_DIM)])
        v = merge(heads[:, :, pl.ds(pl.multiple_of(base + 2 * HEAD_DIM, HEAD_DIM), HEAD_DIM)])
        sc = lax.dot_general(q, key, (((1,), (1,)), ((), ())), preferred_element_type=F32)
        sc = sc * HEAD_DIM ** (-0.5)
        e = jnp.exp(sc - jnp.max(sc, axis=-1, keepdims=True))
        w = (e / jnp.sum(e, axis=-1, keepdims=True)).astype(BF16)
        o = jnp.dot(w, v, preferred_element_type=F32).astype(BF16)
        att[:, pl.ds(pl.multiple_of(h * HEAD_DIM, HEAD_DIM), HEAD_DIM)] = o
        return carry

    if WEIGHTS < 0:
        spread_weights()
    for g, (first, count) in enumerate(groups):
        own_heads[g].wait()
        for c in q_copies[g]:
            c.wait_recv()
        if g == min(WEIGHTS, len(groups) - 1):
            spread_weights()
        lax.fori_loop(first, first + count, one_head, 0)
    wout_copy.wait()

    tile = tile_of(width, 512)
    wide = tile_of(wcols, 512)
    state = {}
    batches = batches_of(n_c)

    def project_all():
        def step(t, carry):
            c0 = pl.ds(pl.multiple_of(t * tile, 128), tile)
            y = jnp.dot(att[...], wout_v[:, c0], preferred_element_type=F32)
            y = y.reshape(units, seq_n, unit, tile).astype(BF16)
            for u in range(units):
                part[:, u, :, c0] = y[u]
            return carry

        lax.fori_loop(0, width // tile, step, 0)

    def reduce(c):
        u0, u1 = chunks[c]
        n = u1 - u0
        us = pl.ds(u0, n)
        if not line:
            state["rs", c] = [
                start(push(
                    part.at[lax.rem(s + k, seq_n), us], rs_in.at[s, us],
                    rs_s.at[c, k], rs_r.at[c, k], (d, lax.rem(s + k, seq_n)),
                ))
                for k in order
            ]
            return
        pair = push(
            part.at[pl.ds(lo, 2), us], rs_in.at[pl.ds(lo, 2), us], rs_s.at[c, 1], rs_r.at[c, 1], (d, beside)
        )
        ends_sent.append(pair)
        state["pair", c] = pair

        @pl.when(jnp.logical_not(middle))
        def _():
            pair.start()

        state["rs", c] = [
            start(push(part.at[beside, us], rs_in.at[beside, us], rs_s.at[c, 0], rs_r.at[c, 0], (d, beside)))
        ]

    def relay_sum(c):
        if not line:
            return
        u0, u1 = chunks[c]
        us = pl.ds(u0, u1 - u0)
        across = [
            push(fwd.at[z - lo, us], rs_x.at[us], x_s.at[c, i], x_r.at[c], (d, z))
            for i, z in enumerate((mirror, mirror_beside))
        ]
        middle_sent.extend(across)
        state["rs", c].append(across[0])

        @pl.when(middle)
        def _():
            state["pair", c].wait_recv()
            for i in range(2):
                for u in range(u0, u1):
                    fwd[i, u] = (part[lo + i, u].astype(F32) + rs_in[lo + i, u].astype(F32)).astype(BF16)
            for cp in across:
                cp.start()

    def update(c):
        u0, u1 = chunks[c]
        if c == 0:
            hid_copy.wait()
        for cp in state["rs", c]:
            cp.wait_recv()
        for u in range(u0, u1):
            kept = []
            squares = jnp.zeros((unit, piece), F32)
            for j in range(dom_n):
                c0 = slice(j * piece, (j + 1) * piece)
                total = part[s, u, :, c0].astype(F32)
                if line:
                    total = total + rs_in[s, u, :, c0].astype(F32) + rs_x[u, :, c0].astype(F32)
                else:
                    for k in range(1, seq_n):
                        total = total + rs_in[lax.rem(s + k, seq_n), u, :, c0].astype(F32)
                x = (hid_v[u, :, c0].astype(F32) + gate_ref[:, c0] * total).astype(BF16)
                pieces_h[j, u] = x
                x = x.astype(F32)
                squares = squares + x * x
                kept.append(x)
            inv = lax.rsqrt(jnp.sum(squares, axis=-1, keepdims=True) / width + 1e-06)
            for j in range(dom_n):
                c0 = slice(j * piece, (j + 1) * piece)
                pieces_n[j, u] = (kept[j] * inv * (1.0 + scale_ref[:, c0])).astype(BF16)
        state["n", c] = [
            start(push(
                pieces_n.at[lax.rem(d + k, dom_n), pl.ds(u0, u1 - u0)], arrived[c].at[d],
                n_s.at[c, k], n_r.at[c, k], (lax.rem(d + k, dom_n), s),
            ))
            for k in range(1, dom_n)
        ]
        arrived[c][d] = pieces_n[d, u0:u1]
        state.setdefault("h", []).extend(
            start(push(
                pieces_h.at[lax.rem(d + k, dom_n), pl.ds(u0, u1 - u0)], arrived_h.at[d, pl.ds(u0, u1 - u0)],
                h_s.at[c, k], h_r.at[c, k], (lax.rem(d + k, dom_n), s),
            ))
            for k in range(1, dom_n)
        )
        arrived_h[d, u0:u1] = pieces_h[d, u0:u1]

    def route(c):
        u0, u1 = chunks[c]
        for cp in state["n", c]:
            cp.wait_recv()
        for p in range(dom_n):
            z_all[p // 2 // cx, p // 2 % cx, p % 2, s, u0:u1] = arrived[c][anc_ref[p]]

        def block(z):
            return z_all.at[:, :, :, z, pl.ds(u0, u1 - u0)]

        def give(z, to, i):
            return push(block(z), block(z), z_s.at[c, i], z_r.at[c, i], (d, to))

        if not line:
            state["z", c] = [start(give(s, lax.rem(s + k, seq_n), k)) for k in order]
            return
        state["z1", c] = [start(give(s, beside, 0)), start(give(s, mirror, 1))]
        onward = [
            push(block(z), block(z), z_s.at[c, 2 + i], z_r.at[c, 2], (d, to))
            for i, (z, to) in enumerate(((beside, mirror), (mirror, beside)))
        ]
        middle_sent.extend(onward)
        state["onward", c] = onward
        state["z", c] = onward[:1]
        hand(c, 0, s)

    def relay_rows(c):
        if not line:
            return
        for i, (cp, after, z) in enumerate(zip(state["z1", c], state["onward", c], (beside, mirror))):
            cp.wait_recv()

            @pl.when(middle)
            def _(after=after):
                after.start()

            hand(c, 1 + i, z)

    def route_hidden():
        for cp in state["h"]:
            cp.wait_recv()
        for p in range(dom_n):
            routed_h[p] = arrived_h[anc_ref[p]]
        state["b"] = [
            start(push(
                routed_h.at[lax.rem(d + k, dom_n)], landed.at[d],
                b_s.at[k], b_r.at[k], (lax.rem(d + k, dom_n), s),
            ))
            for k in range(1, dom_n)
        ]
        landed[d] = routed_h[d]

    def finish_hidden():
        for cp in state["b"]:
            cp.wait_recv()
        for j in range(dom_n):
            nh_ref[:, :, j * piece:(j + 1) * piece] = landed[j]

    def hand(c, b, z):
        u0, u1 = chunks[c]
        us = pl.ds(u0, u1 - u0)
        zs = slice(None) if z is None else z
        copies = state.setdefault(("l", c), [])
        for q in range(cy):
            for kk in range(2):
                if q + kk:
                    r, k, i = lax.rem(row + q, cy), core + kk - 2 * kk * core, q * 2 + kk
                    copies.append(start(push(
                        z_all.at[r, :, k, zs, us], lhs_a.at[slot_a, :, zs, us],
                        la_s.at[c, b, i], la_r.at[c, b, i], dev(r, col, k),
                    )))
        for q in range(cx):
            for kk in range(2):
                if q + kk:
                    r, k, i = lax.rem(col + q, cx), core + kk - 2 * kk * core, q * 2 + kk
                    copies.append(start(push(
                        z_all.at[:, r, k, zs, us], lhs_b.at[slot_b, :, zs, us],
                        lb_s.at[c, b, i], lb_r.at[c, b, i], dev(row, r, k),
                    )))

    def hand_out(c):
        u0, u1 = chunks[c]
        us = pl.ds(u0, u1 - u0)
        for cp in state["z", c]:
            cp.wait_recv()
        if line:
            hand(c, 3, mirror_beside)
        else:
            hand(c, 0, None)
        state["oa", c] = keep(z_all.at[row, :, core, :, us], lhs_a.at[slot_a, :, :, us], own_sem.at[c, 0])
        state["ob", c] = keep(z_all.at[:, col, core, :, us], lhs_b.at[slot_b, :, :, us], own_sem.at[c, 1])

    def multiply(g):
        c0, c1 = batches[g]
        c = g
        u0, u1 = chunks[c0][0], chunks[c1 - 1][1]
        n = u1 - u0
        m = seq_n * n * unit
        if c == 0:
            own_a.wait()
            own_b.wait()
            for cp in mate_copies:
                cp.wait_recv()
        for i in range(c0, c1):
            state["oa", i].wait()
            state["ob", i].wait()
            for cp in state["l", i]:
                cp.wait_recv()
        halves = (
            (lhs_a, act_a, w_a, snd_a, rcv_a, oa_s, oa_r, col, cx),
            (lhs_b, act_b, w_b, snd_b, rcv_b, ob_s, ob_r, row, cy),
        )
        for lhs, act, w, snd, rcv, ss, rr, here, many in halves:
            for q in range(many):
                for j in range(lhs.shape[0]):
                    x = lhs[j, lax.rem(here + q, many), :, u0:u1].astype(F32)
                    act[q * m:(q + 1) * m, j * piece:(j + 1) * piece] = x.reshape(m, piece).astype(BF16)
        for t in range(wcols // wide):
            state["o", c, t] = []
            for half, (lhs, act, w, snd, rcv, ss, rr, here, many) in enumerate(halves):
                t0 = slice(t * wide, (t + 1) * wide)
                y = jnp.dot(act[:many * m, :], w[:, t0], preferred_element_type=F32)
                y = y.reshape(many, seq_n, n, unit, wide)
                acc[:, u0:u1, :, half * wcols + t * wide:half * wcols + (t + 1) * wide] = y[0]
                for q in range(1, many):
                    snd[q - 1, :, u0:u1, :, t0] = y[q].astype(BF16)
                    to = lax.rem(here + q, many)
                    block = (q - 1, slice(None), pl.ds(u0, n), slice(None), pl.ds(t * wide, wide))
                    state["o", c, t].append(start(push(
                        snd.at[block], rcv.at[block], ss.at[c, q, t], rr.at[c, q, t],
                        dev(row, to, core) if half == 0 else dev(to, col, core),
                    )))

    def finish(g):
        c = g
        u0, u1 = chunks[batches[g][0]][0], chunks[batches[g][1] - 1][1]
        for t in range(wcols // wide):
            for cp in state["o", c, t]:
                cp.wait_recv()
            for half, (rcv, many) in enumerate(((rcv_a, cx), (rcv_b, cy))):
                o0 = slice(half * wcols + t * wide, half * wcols + (t + 1) * wide)
                y = acc[:, u0:u1, :, o0]
                for q in range(1, many):
                    y = y + rcv[q - 1, :, u0:u1, :, t * wide:(t + 1) * wide].astype(F32)
                out_ref[:, u0:u1, :, o0] = y.astype(BF16)

    project_all()
    for c in range(min(AHEAD, n_c)):
        reduce(c)
    stages = (relay_sum, update, route, relay_rows, hand_out)
    last = {b[1] - 1: g for g, b in enumerate(batches)}
    for t in range(n_c + OFFSETS[-1]):
        if t + AHEAD < n_c:
            reduce(t + AHEAD)
        for off, stage in zip(OFFSETS, stages):
            c = t - off
            if 0 <= c < n_c:
                stage(c)
            if c == n_c - 1 and stage is route:
                route_hidden()
            if c == n_c - 1 and stage is hand_out:
                finish_hidden()
        if t - OFFSETS[5] in last:
            multiply(last[t - OFFSETS[5]])
        if t - OFFSETS[6] in last:
            finish(last[t - OFFSETS[6]])
        if t == FORWARD:
            forward_weights()
    for c in sent:
        c.wait_send()
    if line:
        @pl.when(middle)
        def _():
            for c in middle_sent:
                c.wait_send()

        @pl.when(jnp.logical_not(middle))
        def _():
            for c in ends_sent:
                c.wait_send()


def body(dom_n, seq_n, hidden, qkv, w_out, gate, next_scale, ancestors, w_next):
    _, rows, width = hidden.shape
    unit = unit_of(rows)
    units = rows // unit
    chunks = chunks_of(units)
    n_c = len(chunks)
    cols = qkv.shape[2] // seq_n
    seq_len = rows * seq_n
    out_cols = w_next.shape[1]
    wcols = out_cols // 2
    att_cols = w_out.shape[0]
    cy, cx = grid_of(dom_n)
    piece = width // dom_n
    n_t = wcols // tile_of(wcols, 512)
    n_g = len(groups_of(cols // (3 * HEAD_DIM)))
    most = max(chunks[c1 - 1][1] - chunks[c0][0] for c0, c1 in batches_of(n_c)) * seq_n * unit
    sem = pltpu.SemaphoreType.DMA
    any_spec = pl.BlockSpec(memory_space=pl.ANY)
    vmem = pl.BlockSpec(memory_space=pltpu.VMEM)

    def buf(*shape, dtype=BF16):
        return pltpu.VMEM(shape, dtype)

    nh, out = pl.pallas_call(
        functools.partial(kernel, dom_n, seq_n, chunks),
        out_shape=(
            jax.ShapeDtypeStruct((units, unit, width), BF16),
            jax.ShapeDtypeStruct((seq_n, units, unit, out_cols), BF16),
        ),
        in_specs=[
            pl.BlockSpec(memory_space=pltpu.SMEM), any_spec, any_spec, any_spec, vmem, vmem, any_spec,
        ],
        out_specs=(vmem, vmem),
        scratch_shapes=[
            buf(seq_n, rows, cols),
            buf(att_cols, width),
            buf(units, unit, width),
            buf(seq_len, att_cols),
            buf(seq_n, units, unit, width),
            buf(seq_n, units, unit, width),
            buf(units, unit, width),
            buf(2, units, unit, width),
            buf(dom_n, units, unit, piece),
            buf(dom_n, units, unit, piece),
            *[buf(dom_n, u1 - u0, unit, piece) for u0, u1 in chunks],
            buf(dom_n, units, unit, piece),
            buf(dom_n, units, unit, piece),
            buf(dom_n, units, unit, piece),
            buf(cy, cx, 2, seq_n, units, unit, piece),
            buf(2 * cy, cx, seq_n, units, unit, piece),
            buf(2 * cx, cy, seq_n, units, unit, piece),
            buf(cx * most, 2 * cy * piece),
            buf(cy * most, 2 * cx * piece),
            buf(2 * cy * w_next.shape[0], wcols),
            buf(2 * cx * w_next.shape[0], wcols),
            buf(seq_n, units, unit, out_cols, dtype=F32),
            buf(max(cx - 1, 1), seq_n, units, unit, wcols),
            buf(max(cy - 1, 1), seq_n, units, unit, wcols),
            buf(max(cx - 1, 1), seq_n, units, unit, wcols),
            buf(max(cy - 1, 1), seq_n, units, unit, wcols),
            sem((4 + n_g,)),
            sem((n_g, seq_n)), sem((n_g, seq_n)),
            sem((n_c, seq_n)), sem((n_c, seq_n)),
            sem((n_c, 2)), sem((n_c,)),
            sem((n_c, dom_n)), sem((n_c, dom_n)),
            sem((n_c, seq_n)), sem((n_c, seq_n)),
            sem((n_c, 4, 2 * cy)), sem((n_c, 4, 2 * cy)),
            sem((n_c, 4, 2 * cx)), sem((n_c, 4, 2 * cx)),
            sem((n_c, cx, n_t)), sem((n_c, cx, n_t)),
            sem((n_c, cy, n_t)), sem((n_c, cy, n_t)),
            sem((n_c, dom_n)), sem((n_c, dom_n)),
            sem((dom_n,)), sem((dom_n,)),
            sem((cy,)), sem((cy,)),
            sem((cx,)), sem((cx,)),
            sem((cy,)), sem((cy,)),
            sem((cx,)), sem((cx,)),
            sem((n_c, 2)),
        ],
        compiler_params=pltpu.CompilerParams(
            collective_id=0, has_side_effects=True, vmem_limit_bytes=60 * 1024 * 1024
        ),
    )(
        ancestors, hidden.reshape(units, unit, width), qkv, w_out, gate[None], next_scale[None], w_next
    )
    nh, out = settle(nh, out)
    return nh.reshape(1, rows, width), out.reshape(1, seq_len, out_cols)


def settle_kernel(a_ref, b_ref, a_out, b_out, sem):
    copies = [pltpu.make_async_copy(a_ref, a_out, sem.at[0])]
    n = b_ref.shape[0]
    for i in range(n):
        copies.append(pltpu.make_async_copy(b_ref.at[i], b_out.at[i], sem.at[1 + i]))
    for c in copies:
        c.start()
    for c in copies:
        c.wait()


def settle(a, b):
    spec = pl.BlockSpec(memory_space=pltpu.VMEM)
    out = pl.BlockSpec(memory_space=pl.ANY)
    return pl.pallas_call(
        settle_kernel,
        out_shape=(jax.ShapeDtypeStruct(a.shape, a.dtype), jax.ShapeDtypeStruct(b.shape, b.dtype)),
        in_specs=[spec, spec],
        out_specs=(out, out),
        scratch_shapes=[pltpu.SemaphoreType.DMA((1 + b.shape[0],))],
    )(a, b)


def solution(mesh):
    in_specs = (
        P("dom", "seq", None),
        P("dom", "seq", None),
        P("seq", None),
        P(),
        P(),
        P(),
        P("dom", "seq"),
    )
    out_specs = (P("dom", "seq", None), P("dom", None, "seq"))
    return jax.shard_map(
        functools.partial(body, mesh.shape["dom"], mesh.shape["seq"]),
        mesh=mesh, in_specs=in_specs, out_specs=out_specs, check_vma=False,
    )
```

```python
import functools

import jax
import jax.numpy as jnp
from jax import lax
from jax.experimental import pallas as pl
from jax.experimental.pallas import tpu as pltpu
from jax.sharding import PartitionSpec as P

HEAD_DIM = 128
MESH = pl.DeviceIdType.MESH
F32 = jnp.float32
BF16 = jnp.bfloat16
UNIT = 8
SPLIT = (2, 2, 1)
BATCHES = (1, 1, 1)
OFFSETS = (0, 1, 2, 3, 4, 5, 6)
AHEAD = 1
DIRECT = 0
FORWARD = 1
TAIL_SHARE = 4


def tile_of(width, most):
    return max(t for t in range(128, most + 1, 128) if width % t == 0)


def grid_of(dom_n):
    chips = dom_n // 2
    cx = max(c for c in range(1, chips + 1) if chips % c == 0 and c * c <= chips)
    return chips // cx, cx


def unit_of(rows):
    return UNIT if rows % UNIT == 0 else rows


def chunks_of(units):
    edges = [0]
    for n in SPLIT:
        edges.append(edges[-1] + n)
    cuts = sorted({units * e // edges[-1] for e in edges})
    return list(zip(cuts[:-1], cuts[1:]))


def batches_of(n_c):
    edges = [0]
    for n in BATCHES:
        edges.append(min(edges[-1] + n, n_c))
    edges[-1] = n_c
    cuts = sorted(set(edges))
    return list(zip(cuts[:-1], cuts[1:]))


def groups_of(heads):
    tail = max(heads // TAIL_SHARE, 1)
    return [(0, heads - tail), (heads - tail, tail)] if heads > 1 else [(0, 1)]


def kernel(dom_n, seq_n, chunks, *refs):
    n_c = len(chunks)
    (anc_ref, hidden_ref, qkv_ref, wout_ref, gate_ref, scale_ref, wnext_ref, nh_ref, out_ref,
     heads, wout_v, hid_v, att, part, rs_in, rs_x, fwd, pieces_n, pieces_h) = refs[:19]
    arrived = refs[19:19 + n_c]
    (arrived_h, routed_h, landed, z_all, lhs_a, lhs_b, act_a, act_b, w_a, w_b, acc, snd_a, snd_b, rcv_a, rcv_b,
     loc_sem, q_s, q_r, rs_s, rs_r, x_s, x_r, n_s, n_r, z_s, z_r, la_s, la_r, lb_s, lb_r, oa_s, oa_r, ob_s, ob_r,
     h_s, h_r, b_s, b_r, wa_s, wa_r, wb_s, wb_r, ma_s, ma_r, mb_s, mb_r, own_sem, out_sem, nh_v, out_v, head_sum) = refs[19 + n_c:]

    cy, cx = grid_of(dom_n)
    d = lax.axis_index("dom")
    s = lax.axis_index("seq")
    core = lax.rem(d, 2)
    chip = d // 2
    col = lax.rem(chip, cx)
    row = chip // cx
    mate = d + 1 - 2 * core
    units, unit, width = hid_v.shape
    seq_len = seq_n * units * unit
    cols = heads.shape[2]
    head_n = cols // (3 * HEAD_DIM)
    groups = groups_of(head_n)
    spans = [(first * 3 * HEAD_DIM, count * 3 * HEAD_DIM) for first, count in groups]
    wrows = wnext_ref.shape[0]
    wcols = w_a.shape[1]
    piece = width // dom_n

    def dev(r, c, k):
        return ((r * cx + c) * 2 + k, s)

    def push(src, dst, send, recv, to):
        return pltpu.make_async_remote_copy(
            src_ref=src, dst_ref=dst, send_sem=send, recv_sem=recv, device_id=to, device_id_type=MESH
        )

    def keep(src, dst, sem):
        c = pltpu.make_async_copy(src, dst, sem)
        c.start()
        return c

    def wslot(ref, slot):
        return ref.at[pl.ds(pl.multiple_of(slot * wrows, 16), wrows), :]

    slot_a = row * 2 + core
    slot_b = col * 2 + core
    src_a = wnext_ref.at[:, pl.ds(0, wcols)]
    src_b = wnext_ref.at[:, pl.ds(wcols, wcols)]

    def head_src(to, g):
        return qkv_ref.at[0, :, pl.ds(pl.multiple_of(to * cols + spans[g][0], 128), spans[g][1])]

    own_heads = [
        keep(head_src(s, g), heads.at[s, :, pl.ds(*spans[g])], loc_sem.at[4 + g])
        for g in range(len(groups))
    ]
    wout_copy = keep(wout_ref, wout_v, loc_sem.at[0])
    hid_copy = keep(hidden_ref, hid_v, loc_sem.at[1])
    own_a = keep(src_a, wslot(w_a, slot_a), loc_sem.at[2])
    own_b = keep(src_b, wslot(w_b, slot_b), loc_sem.at[3])

    barrier = pltpu.get_barrier_semaphore()
    for k in range(1, seq_n):
        pl.semaphore_signal(barrier, inc=1, device_id=(d, lax.rem(s + k, seq_n)), device_id_type=MESH)
    for k in range(1, dom_n):
        pl.semaphore_signal(barrier, inc=1, device_id=(lax.rem(d + k, dom_n), s), device_id_type=MESH)
    pl.semaphore_wait(barrier, seq_n - 1 + dom_n - 1)

    line = seq_n == 4
    if line:
        beside = s + 1 - 2 * lax.rem(s, 2)
        mirror = 3 - s
        mirror_beside = mirror + 1 - 2 * lax.rem(mirror, 2)
        lo = 2 - 2 * (s // 2)
        middle = s * (3 - s) == 2
    sent = []
    ends_sent = []
    middle_sent = []

    def start(c):
        c.start()
        sent.append(c)
        return c

    order = sorted(range(1, seq_n), key=lambda k: -min(k, seq_n - k))
    q_copies = []
    for g in range(len(groups)):
        q_copies.append([
            start(push(
                head_src(lax.rem(s + k, seq_n), g), heads.at[s, :, pl.ds(*spans[g])],
                q_s.at[g, k], q_r.at[g, k], (d, lax.rem(s + k, seq_n)),
            ))
            for k in order
        ])

    wa_copies, wb_copies, mate_copies = [], [], []

    def spread_weights():
        wa_copies[:] = [
            start(push(src_a, wslot(w_a, slot_a), wa_s.at[q], wa_r.at[q], dev(lax.rem(row + q, cy), col, core)))
            for q in range(1, cy)
        ]
        wb_copies[:] = [
            start(push(src_b, wslot(w_b, slot_b), wb_s.at[q], wb_r.at[q], dev(row, lax.rem(col + q, cx), core)))
            for q in range(1, cx)
        ]
        mate_copies[:] = [
            start(push(src_a, wslot(w_a, slot_a), ma_s.at[0], ma_r.at[0], (mate, s))),
            start(push(src_b, wslot(w_b, slot_b), mb_s.at[0], mb_r.at[0], (mate, s))),
        ]

    def forward_weights():
        for q in range(1, cy):
            wa_copies[q - 1].wait_recv()
            slot = wslot(w_a, lax.rem(row + cy - q, cy) * 2 + core)
            mate_copies.append(start(push(slot, slot, ma_s.at[q], ma_r.at[q], (mate, s))))
        for q in range(1, cx):
            wb_copies[q - 1].wait_recv()
            slot = wslot(w_b, lax.rem(col + cx - q, cx) * 2 + core)
            mate_copies.append(start(push(slot, slot, mb_s.at[q], mb_r.at[q], (mate, s))))

    def merge(x):
        return x.astype(F32).reshape(seq_len, x.shape[-1]).astype(BF16)

    def unit_major(x):
        x = x.astype(F32).reshape(seq_n, units, unit, x.shape[-1])
        return jnp.transpose(x, (1, 0, 2, 3)).reshape(seq_len, x.shape[-1]).astype(BF16)

    def one_head(h, carry):
        base = pl.multiple_of(h * 3 * HEAD_DIM, HEAD_DIM)
        q = unit_major(heads[:, :, pl.ds(base, HEAD_DIM)])
        key = merge(heads[:, :, pl.ds(pl.multiple_of(base + HEAD_DIM, HEAD_DIM), HEAD_DIM)])
        v = merge(heads[:, :, pl.ds(pl.multiple_of(base + 2 * HEAD_DIM, HEAD_DIM), HEAD_DIM)])
        sc = lax.dot_general(q, key, (((1,), (1,)), ((), ())), preferred_element_type=F32)
        sc = sc * HEAD_DIM ** (-0.5)
        e = jnp.exp(sc - jnp.max(sc, axis=-1, keepdims=True))
        w = (e / jnp.sum(e, axis=-1, keepdims=True)).astype(BF16)
        o = jnp.dot(w, v, preferred_element_type=F32).astype(BF16)
        att[:, pl.ds(pl.multiple_of(h * HEAD_DIM, HEAD_DIM), HEAD_DIM)] = o
        return carry

    tile = tile_of(width, 512)
    wide = tile_of(wcols, 512)
    state = {}
    kept_out = []
    batches = batches_of(n_c)

    def project(g):
        k0, k1 = groups[g][0] * HEAD_DIM, sum(groups[g]) * HEAD_DIM

        def step(t, carry):
            c0 = pl.ds(pl.multiple_of(t * tile, 128), tile)
            y = jnp.dot(att[:, k0:k1], wout_v[k0:k1, c0], preferred_element_type=F32)
            if g > 0:
                y = y + head_sum[:, c0]
            if g < len(groups) - 1:
                head_sum[:, c0] = y
            else:
                y = y.reshape(units, seq_n, unit, tile).astype(BF16)
                for u in range(units):
                    part[:, u, :, c0] = y[u]
            return carry

        lax.fori_loop(0, width // tile, step, 0)

    def reduce(c):
        u0, u1 = chunks[c]
        n = u1 - u0
        us = pl.ds(u0, n)
        if not line:
            state["rs", c] = [
                start(push(
                    part.at[lax.rem(s + k, seq_n), us], rs_in.at[s, us],
                    rs_s.at[c, k], rs_r.at[c, k], (d, lax.rem(s + k, seq_n)),
                ))
                for k in order
            ]
            return
        pair = push(
            part.at[pl.ds(lo, 2), us], rs_in.at[pl.ds(lo, 2), us], rs_s.at[c, 1], rs_r.at[c, 1], (d, beside)
        )
        ends_sent.append(pair)
        state["pair", c] = pair

        @pl.when(jnp.logical_not(middle))
        def _():
            pair.start()

        state["rs", c] = [
            start(push(part.at[beside, us], rs_in.at[beside, us], rs_s.at[c, 0], rs_r.at[c, 0], (d, beside)))
        ]

    def relay_sum(c):
        if not line:
            return
        u0, u1 = chunks[c]
        us = pl.ds(u0, u1 - u0)
        across = [
            push(fwd.at[z - lo, us], rs_x.at[us], x_s.at[c, i], x_r.at[c], (d, z))
            for i, z in enumerate((mirror, mirror_beside))
        ]
        middle_sent.extend(across)
        state["rs", c].append(across[0])

        @pl.when(middle)
        def _():
            state["pair", c].wait_recv()
            for i in range(2):
                for u in range(u0, u1):
                    fwd[i, u] = (part[lo + i, u].astype(F32) + rs_in[lo + i, u].astype(F32)).astype(BF16)
            for cp in across:
                cp.start()

    def update(c):
        u0, u1 = chunks[c]
        if c == 0:
            hid_copy.wait()
        for cp in state["rs", c]:
            cp.wait_recv()
        for u in range(u0, u1):
            kept = []
            squares = jnp.zeros((unit, piece), F32)
            for j in range(dom_n):
                c0 = slice(j * piece, (j + 1) * piece)
                total = part[s, u, :, c0].astype(F32)
                if line:
                    total = total + rs_in[s, u, :, c0].astype(F32) + rs_x[u, :, c0].astype(F32)
                else:
                    for k in range(1, seq_n):
                        total = total + rs_in[lax.rem(s + k, seq_n), u, :, c0].astype(F32)
                x = (hid_v[u, :, c0].astype(F32) + gate_ref[:, c0] * total).astype(BF16)
                pieces_h[j, u] = x
                x = x.astype(F32)
                squares = squares + x * x
                kept.append(x)
            inv = lax.rsqrt(jnp.sum(squares, axis=-1, keepdims=True) / width + 1e-06)
            for j in range(dom_n):
                c0 = slice(j * piece, (j + 1) * piece)
                pieces_n[j, u] = (kept[j] * inv * (1.0 + scale_ref[:, c0])).astype(BF16)
        state["n", c] = [
            start(push(
                pieces_n.at[lax.rem(d + k, dom_n), pl.ds(u0, u1 - u0)], arrived[c].at[d],
                n_s.at[c, k], n_r.at[c, k], (lax.rem(d + k, dom_n), s),
            ))
            for k in range(1, dom_n)
        ]
        arrived[c][d] = pieces_n[d, u0:u1]
        state.setdefault("h", []).extend(
            start(push(
                pieces_h.at[lax.rem(d + k, dom_n), pl.ds(u0, u1 - u0)], arrived_h.at[d, pl.ds(u0, u1 - u0)],
                h_s.at[c, k], h_r.at[c, k], (lax.rem(d + k, dom_n), s),
            ))
            for k in range(1, dom_n)
        )
        arrived_h[d, u0:u1] = pieces_h[d, u0:u1]

    def route(c):
        u0, u1 = chunks[c]
        for cp in state["n", c]:
            cp.wait_recv()
        for p in range(dom_n):
            z_all[p // 2 // cx, p // 2 % cx, p % 2, s, u0:u1] = arrived[c][anc_ref[p]]

        def block(z):
            return z_all.at[:, :, :, z, pl.ds(u0, u1 - u0)]

        def give(z, to, i):
            return push(block(z), block(z), z_s.at[c, i], z_r.at[c, i], (d, to))

        if not line:
            state["z", c] = [start(give(s, lax.rem(s + k, seq_n), k)) for k in order]
            return
        state["z1", c] = [start(give(s, beside, 0)), start(give(s, mirror, 1))]
        if c >= n_c - DIRECT:
            state["onward", c] = None
            state["z", c] = [start(give(s, mirror_beside, 2))]
            hand(c, 0, s)
            return
        onward = [
            push(block(z), block(z), z_s.at[c, 2 + i], z_r.at[c, 2], (d, to))
            for i, (z, to) in enumerate(((beside, mirror), (mirror, beside)))
        ]
        middle_sent.extend(onward)
        state["onward", c] = onward
        state["z", c] = onward[:1]
        hand(c, 0, s)

    def relay_rows(c):
        if not line:
            return
        for i, (cp, z) in enumerate(zip(state["z1", c], (beside, mirror))):
            cp.wait_recv()
            if state["onward", c] is not None:
                after = state["onward", c][i]

                @pl.when(middle)
                def _(after=after):
                    after.start()

            hand(c, 1 + i, z)

    def route_hidden():
        for cp in state["h"]:
            cp.wait_recv()
        for p in range(dom_n):
            routed_h[p] = arrived_h[anc_ref[p]]
        state["b"] = [
            start(push(
                routed_h.at[lax.rem(d + k, dom_n)], landed.at[d],
                b_s.at[k], b_r.at[k], (lax.rem(d + k, dom_n), s),
            ))
            for k in range(1, dom_n)
        ]
        landed[d] = routed_h[d]

    def finish_hidden():
        for cp in state["b"]:
            cp.wait_recv()
        for j in range(dom_n):
            nh_v[:, :, j * piece:(j + 1) * piece] = landed[j]
        kept_out.append(keep(nh_v, nh_ref, loc_sem.at[0]))

    def hand(c, b, z):
        u0, u1 = chunks[c]
        us = pl.ds(u0, u1 - u0)
        zs = slice(None) if z is None else z
        copies = state.setdefault(("l", c), [])
        for q in range(cy):
            for kk in range(2):
                if q + kk:
                    r, k, i = lax.rem(row + q, cy), core + kk - 2 * kk * core, q * 2 + kk
                    copies.append(start(push(
                        z_all.at[r, :, k, zs, us], lhs_a.at[slot_a, :, zs, us],
                        la_s.at[c, b, i], la_r.at[c, b, i], dev(r, col, k),
                    )))
        for q in range(cx):
            for kk in range(2):
                if q + kk:
                    r, k, i = lax.rem(col + q, cx), core + kk - 2 * kk * core, q * 2 + kk
                    copies.append(start(push(
                        z_all.at[:, r, k, zs, us], lhs_b.at[slot_b, :, zs, us],
                        lb_s.at[c, b, i], lb_r.at[c, b, i], dev(row, r, k),
                    )))

    def hand_out(c):
        u0, u1 = chunks[c]
        us = pl.ds(u0, u1 - u0)
        for cp in state["z", c]:
            cp.wait_recv()
        if line:
            hand(c, 3, mirror_beside)
        else:
            hand(c, 0, None)
        state["oa", c] = keep(z_all.at[row, :, core, :, us], lhs_a.at[slot_a, :, :, us], own_sem.at[c, 0])
        state["ob", c] = keep(z_all.at[:, col, core, :, us], lhs_b.at[slot_b, :, :, us], own_sem.at[c, 1])

    def multiply(g):
        c0, c1 = batches[g]
        c = g
        u0, u1 = chunks[c0][0], chunks[c1 - 1][1]
        n = u1 - u0
        m = seq_n * n * unit
        if c == 0:
            own_a.wait()
            own_b.wait()
            for cp in mate_copies:
                cp.wait_recv()
        for i in range(c0, c1):
            state["oa", i].wait()
            state["ob", i].wait()
            for cp in state["l", i]:
                cp.wait_recv()
        halves = (
            (lhs_a, act_a, w_a, snd_a, rcv_a, oa_s, oa_r, col, cx),
            (lhs_b, act_b, w_b, snd_b, rcv_b, ob_s, ob_r, row, cy),
        )
        for lhs, act, w, snd, rcv, ss, rr, here, many in halves:
            for q in range(many):
                for j in range(lhs.shape[0]):
                    x = lhs[j, lax.rem(here + q, many), :, u0:u1].astype(F32)
                    act[q * m:(q + 1) * m, j * piece:(j + 1) * piece] = x.reshape(m, piece).astype(BF16)
        for t in range(wcols // wide):
            state["o", c, t] = []
            for half, (lhs, act, w, snd, rcv, ss, rr, here, many) in enumerate(halves):
                t0 = slice(t * wide, (t + 1) * wide)
                y = jnp.dot(act[:many * m, :], w[:, t0], preferred_element_type=F32)
                y = y.reshape(many, seq_n, n, unit, wide)
                acc[:, u0:u1, :, half * wcols + t * wide:half * wcols + (t + 1) * wide] = y[0]
                for q in range(1, many):
                    snd[q - 1, :, u0:u1, :, t0] = y[q].astype(BF16)
                    to = lax.rem(here + q, many)
                    block = (q - 1, slice(None), pl.ds(u0, n), slice(None), pl.ds(t * wide, wide))
                    state["o", c, t].append(start(push(
                        snd.at[block], rcv.at[block], ss.at[c, q, t], rr.at[c, q, t],
                        dev(row, to, core) if half == 0 else dev(to, col, core),
                    )))

    def finish(g):
        c = g
        u0, u1 = chunks[batches[g][0]][0], chunks[batches[g][1] - 1][1]
        for t in range(wcols // wide):
            for cp in state["o", c, t]:
                cp.wait_recv()
            for half, (rcv, many) in enumerate(((rcv_a, cx), (rcv_b, cy))):
                o0 = slice(half * wcols + t * wide, half * wcols + (t + 1) * wide)
                y = acc[:, u0:u1, :, o0]
                for q in range(1, many):
                    y = y + rcv[q - 1, :, u0:u1, :, t * wide:(t + 1) * wide].astype(F32)
                out_v[:, u0:u1, :, o0] = y.astype(BF16)

        kept_out.append(keep(out_v.at[:, pl.ds(u0, u1 - u0)], out_ref.at[:, pl.ds(u0, u1 - u0)], out_sem.at[g]))

    spread_weights()
    for g, (first, count) in enumerate(groups):
        own_heads[g].wait()
        for c in q_copies[g]:
            c.wait_recv()
        lax.fori_loop(first, first + count, one_head, 0)
        if g == 0:
            wout_copy.wait()
        project(g)
    for c in range(min(AHEAD, n_c)):
        reduce(c)
    def drain():
        for c in sent:
            c.wait_send()
        sent.clear()
        if line:
            @pl.when(middle)
            def _():
                for c in middle_sent:
                    c.wait_send()

            @pl.when(jnp.logical_not(middle))
            def _():
                for c in ends_sent:
                    c.wait_send()

    stages = (relay_sum, update, route, relay_rows, hand_out)
    last = {b[1] - 1: g for g, b in enumerate(batches)}
    for t in range(n_c + OFFSETS[-1]):
        if t + AHEAD < n_c:
            reduce(t + AHEAD)
        for off, stage in zip(OFFSETS, stages):
            c = t - off
            if 0 <= c < n_c:
                stage(c)
            if c == n_c - 1 and stage is route:
                route_hidden()
            if c == n_c - 1 and stage is hand_out:
                finish_hidden()
        if t - OFFSETS[5] in last:
            multiply(last[t - OFFSETS[5]])
        if last.get(t - OFFSETS[6], -1) == len(batches) - 1:
            drain()
        if t - OFFSETS[6] in last:
            finish(last[t - OFFSETS[6]])
        if t == FORWARD:
            forward_weights()
    for c in sent:
        c.wait_send()
    for c in kept_out:
        c.wait()


def body(dom_n, seq_n, hidden, qkv, w_out, gate, next_scale, ancestors, w_next):
    _, rows, width = hidden.shape
    unit = unit_of(rows)
    units = rows // unit
    chunks = chunks_of(units)
    n_c = len(chunks)
    cols = qkv.shape[2] // seq_n
    seq_len = rows * seq_n
    out_cols = w_next.shape[1]
    wcols = out_cols // 2
    att_cols = w_out.shape[0]
    cy, cx = grid_of(dom_n)
    piece = width // dom_n
    n_t = wcols // tile_of(wcols, 512)
    n_g = len(groups_of(cols // (3 * HEAD_DIM)))
    most = max(chunks[c1 - 1][1] - chunks[c0][0] for c0, c1 in batches_of(n_c)) * seq_n * unit
    sem = pltpu.SemaphoreType.DMA
    any_spec = pl.BlockSpec(memory_space=pl.ANY)
    vmem = pl.BlockSpec(memory_space=pltpu.VMEM)

    def buf(*shape, dtype=BF16):
        return pltpu.VMEM(shape, dtype)

    nh, out = pl.pallas_call(
        functools.partial(kernel, dom_n, seq_n, chunks),
        out_shape=(
            jax.ShapeDtypeStruct((units, unit, width), BF16),
            jax.ShapeDtypeStruct((seq_n, units, unit, out_cols), BF16),
        ),
        in_specs=[
            pl.BlockSpec(memory_space=pltpu.SMEM), any_spec, any_spec, any_spec, vmem, vmem, any_spec,
        ],
        out_specs=(any_spec, any_spec),
        scratch_shapes=[
            buf(seq_n, rows, cols),
            buf(att_cols, width),
            buf(units, unit, width),
            buf(seq_len, att_cols),
            buf(seq_n, units, unit, width),
            buf(seq_n, units, unit, width),
            buf(units, unit, width),
            buf(2, units, unit, width),
            buf(dom_n, units, unit, piece),
            buf(dom_n, units, unit, piece),
            *[buf(dom_n, u1 - u0, unit, piece) for u0, u1 in chunks],
            buf(dom_n, units, unit, piece),
            buf(dom_n, units, unit, piece),
            buf(dom_n, units, unit, piece),
            buf(cy, cx, 2, seq_n, units, unit, piece),
            buf(2 * cy, cx, seq_n, units, unit, piece),
            buf(2 * cx, cy, seq_n, units, unit, piece),
            buf(cx * most, 2 * cy * piece),
            buf(cy * most, 2 * cx * piece),
            buf(2 * cy * w_next.shape[0], wcols),
            buf(2 * cx * w_next.shape[0], wcols),
            buf(seq_n, units, unit, out_cols, dtype=F32),
            buf(max(cx - 1, 1), seq_n, units, unit, wcols),
            buf(max(cy - 1, 1), seq_n, units, unit, wcols),
            buf(max(cx - 1, 1), seq_n, units, unit, wcols),
            buf(max(cy - 1, 1), seq_n, units, unit, wcols),
            sem((4 + n_g,)),
            sem((n_g, seq_n)), sem((n_g, seq_n)),
            sem((n_c, seq_n)), sem((n_c, seq_n)),
            sem((n_c, 2)), sem((n_c,)),
            sem((n_c, dom_n)), sem((n_c, dom_n)),
            sem((n_c, seq_n)), sem((n_c, seq_n)),
            sem((n_c, 4, 2 * cy)), sem((n_c, 4, 2 * cy)),
            sem((n_c, 4, 2 * cx)), sem((n_c, 4, 2 * cx)),
            sem((n_c, cx, n_t)), sem((n_c, cx, n_t)),
            sem((n_c, cy, n_t)), sem((n_c, cy, n_t)),
            sem((n_c, dom_n)), sem((n_c, dom_n)),
            sem((dom_n,)), sem((dom_n,)),
            sem((cy,)), sem((cy,)),
            sem((cx,)), sem((cx,)),
            sem((cy,)), sem((cy,)),
            sem((cx,)), sem((cx,)),
            sem((n_c, 2)),
            sem((n_c,)),
            buf(units, unit, width),
            buf(seq_n, units, unit, out_cols),
            buf(seq_len, width, dtype=F32),
        ],
        compiler_params=pltpu.CompilerParams(
            collective_id=0, has_side_effects=True, vmem_limit_bytes=60 * 1024 * 1024
        ),
    )(
        ancestors, hidden.reshape(units, unit, width), qkv, w_out, gate[None], next_scale[None], w_next
    )
    nh, out = settle(nh, out)
    return nh.reshape(1, rows, width), out.reshape(1, seq_len, out_cols)


def settle_kernel(a_ref, b_ref, a_out, b_out, a_v, b_v, sem_in, sem_out):
    pairs = [(a_ref, a_v, a_out)] + [(b_ref.at[i], b_v.at[i], b_out.at[i]) for i in range(b_ref.shape[0])]
    reads = [pltpu.make_async_copy(x, v, sem_in.at[i]) for i, (x, v, _) in enumerate(pairs)]
    writes = [pltpu.make_async_copy(v, y, sem_out.at[i]) for i, (_, v, y) in enumerate(pairs)]
    for c in reads:
        c.start()
    for r, w in zip(reads, writes):
        r.wait()
        w.start()
    for c in writes:
        c.wait()


def settle(a, b):
    spec = pl.BlockSpec(memory_space=pl.ANY)
    sems = pltpu.SemaphoreType.DMA((1 + b.shape[0],))
    return pl.pallas_call(
        settle_kernel,
        out_shape=(jax.ShapeDtypeStruct(a.shape, a.dtype), jax.ShapeDtypeStruct(b.shape, b.dtype)),
        in_specs=[spec, spec],
        out_specs=(spec, spec),
        scratch_shapes=[pltpu.VMEM(a.shape, a.dtype), pltpu.VMEM(b.shape, b.dtype), sems, sems],
        compiler_params=pltpu.CompilerParams(vmem_limit_bytes=60 * 1024 * 1024),
    )(a, b)


def solution(mesh):
    in_specs = (
        P("dom", "seq", None),
        P("dom", "seq", None),
        P("seq", None),
        P(),
        P(),
        P(),
        P("dom", "seq"),
    )
    out_specs = (P("dom", "seq", None), P("dom", None, "seq"))
    return jax.shard_map(
        functools.partial(body, mesh.shape["dom"], mesh.shape["seq"]),
        mesh=mesh, in_specs=in_specs, out_specs=out_specs, check_vma=False,
    )
```

```python
import functools

import jax
import jax.numpy as jnp
from jax import lax
from jax.experimental import pallas as pl
from jax.experimental.pallas import tpu as pltpu
from jax.sharding import PartitionSpec as P

HEAD_DIM = 128
MESH = pl.DeviceIdType.MESH
F32 = jnp.float32
BF16 = jnp.bfloat16
UNIT = 8
SPLIT = (2, 2, 1)
BATCHES = (1, 1, 1)
OFFSETS = (0, 1, 2, 3, 4, 5, 6)
AHEAD = 1
DIRECT = 0
FORWARD = 2
TAIL_SHARE = 4


def tile_of(width, most):
    return max(t for t in range(128, most + 1, 128) if width % t == 0)


def grid_of(dom_n):
    chips = dom_n // 2
    cx = max(c for c in range(1, chips + 1) if chips % c == 0 and c * c <= chips)
    return chips // cx, cx


def unit_of(rows):
    return UNIT if rows % UNIT == 0 else rows


def chunks_of(units):
    edges = [0]
    for n in SPLIT:
        edges.append(edges[-1] + n)
    cuts = sorted({units * e // edges[-1] for e in edges})
    return list(zip(cuts[:-1], cuts[1:]))


def batches_of(n_c):
    edges = [0]
    for n in BATCHES:
        edges.append(min(edges[-1] + n, n_c))
    edges[-1] = n_c
    cuts = sorted(set(edges))
    return list(zip(cuts[:-1], cuts[1:]))


def groups_of(heads):
    tail = max(heads // TAIL_SHARE, 1)
    return [(0, heads - tail), (heads - tail, tail)] if heads > 1 else [(0, 1)]


def kernel(dom_n, seq_n, chunks, *refs):
    n_c = len(chunks)
    (anc_ref, hidden_ref, qkv_ref, wout_ref, gate_ref, scale_ref, wnext_ref, nh_ref, out_ref,
     heads, wout_v, hid_v, att, part, rs_in, rs_x, fwd, pieces_n, pieces_h) = refs[:19]
    arrived = refs[19:19 + n_c]
    (arrived_h, routed_h, landed, z_all, lhs_a, lhs_b, act_a, act_b, w_a, w_b, acc, snd_a, snd_b, rcv_a, rcv_b,
     loc_sem, q_s, q_r, rs_s, rs_r, x_s, x_r, n_s, n_r, z_s, z_r, la_s, la_r, lb_s, lb_r, oa_s, oa_r, ob_s, ob_r,
     h_s, h_r, b_s, b_r, wa_s, wa_r, wb_s, wb_r, ma_s, ma_r, mb_s, mb_r, own_sem, out_sem, nh_v, out_v, head_sum) = refs[19 + n_c:]

    cy, cx = grid_of(dom_n)
    d = lax.axis_index("dom")
    s = lax.axis_index("seq")
    core = lax.rem(d, 2)
    chip = d // 2
    col = lax.rem(chip, cx)
    row = chip // cx
    mate = d + 1 - 2 * core
    units, unit, width = hid_v.shape
    seq_len = seq_n * units * unit
    cols = heads.shape[2]
    head_n = cols // (3 * HEAD_DIM)
    groups = groups_of(head_n)
    spans = [(first * 3 * HEAD_DIM, count * 3 * HEAD_DIM) for first, count in groups]
    wrows = wnext_ref.shape[0]
    wcols = w_a.shape[1]
    piece = width // dom_n

    def dev(r, c, k):
        return ((r * cx + c) * 2 + k, s)

    def push(src, dst, send, recv, to):
        return pltpu.make_async_remote_copy(
            src_ref=src, dst_ref=dst, send_sem=send, recv_sem=recv, device_id=to, device_id_type=MESH
        )

    def keep(src, dst, sem):
        c = pltpu.make_async_copy(src, dst, sem)
        c.start()
        return c

    def wslot(ref, slot):
        return ref.at[pl.ds(pl.multiple_of(slot * wrows, 16), wrows), :]

    slot_a = row * 2 + core
    slot_b = col * 2 + core
    src_a = wnext_ref.at[:, pl.ds(0, wcols)]
    src_b = wnext_ref.at[:, pl.ds(wcols, wcols)]

    def head_src(to, g):
        return qkv_ref.at[0, :, pl.ds(pl.multiple_of(to * cols + spans[g][0], 128), spans[g][1])]

    own_heads = [
        keep(head_src(s, g), heads.at[s, :, pl.ds(*spans[g])], loc_sem.at[4 + g])
        for g in range(len(groups))
    ]
    wout_copy = keep(wout_ref, wout_v, loc_sem.at[0])
    hid_copy = keep(hidden_ref, hid_v, loc_sem.at[1])
    own_a = keep(src_a, wslot(w_a, slot_a), loc_sem.at[2])
    own_b = keep(src_b, wslot(w_b, slot_b), loc_sem.at[3])

    barrier = pltpu.get_barrier_semaphore()
    for k in range(1, seq_n):
        pl.semaphore_signal(barrier, inc=1, device_id=(d, lax.rem(s + k, seq_n)), device_id_type=MESH)
    for k in range(1, dom_n):
        pl.semaphore_signal(barrier, inc=1, device_id=(lax.rem(d + k, dom_n), s), device_id_type=MESH)
    pl.semaphore_wait(barrier, seq_n - 1 + dom_n - 1)

    line = seq_n == 4
    if line:
        beside = s + 1 - 2 * lax.rem(s, 2)
        mirror = 3 - s
        mirror_beside = mirror + 1 - 2 * lax.rem(mirror, 2)
        lo = 2 - 2 * (s // 2)
        middle = s * (3 - s) == 2
    sent = []
    ends_sent = []
    middle_sent = []

    def start(c):
        c.start()
        sent.append(c)
        return c

    order = sorted(range(1, seq_n), key=lambda k: -min(k, seq_n - k))
    q_copies = []
    for g in range(len(groups)):
        q_copies.append([
            start(push(
                head_src(lax.rem(s + k, seq_n), g), heads.at[s, :, pl.ds(*spans[g])],
                q_s.at[g, k], q_r.at[g, k], (d, lax.rem(s + k, seq_n)),
            ))
            for k in order
        ])

    wa_copies, wb_copies, mate_copies = [], [], []

    def spread_weights():
        wa_copies[:] = [
            start(push(src_a, wslot(w_a, slot_a), wa_s.at[q], wa_r.at[q], dev(lax.rem(row + q, cy), col, core)))
            for q in range(1, cy)
        ]
        wb_copies[:] = [
            start(push(src_b, wslot(w_b, slot_b), wb_s.at[q], wb_r.at[q], dev(row, lax.rem(col + q, cx), core)))
            for q in range(1, cx)
        ]
        mate_copies[:] = [
            start(push(src_a, wslot(w_a, slot_a), ma_s.at[0], ma_r.at[0], (mate, s))),
            start(push(src_b, wslot(w_b, slot_b), mb_s.at[0], mb_r.at[0], (mate, s))),
        ]

    def forward_weights():
        for q in range(1, cy):
            wa_copies[q - 1].wait_recv()
            slot = wslot(w_a, lax.rem(row + cy - q, cy) * 2 + core)
            mate_copies.append(start(push(slot, slot, ma_s.at[q], ma_r.at[q], (mate, s))))
        for q in range(1, cx):
            wb_copies[q - 1].wait_recv()
            slot = wslot(w_b, lax.rem(col + cx - q, cx) * 2 + core)
            mate_copies.append(start(push(slot, slot, mb_s.at[q], mb_r.at[q], (mate, s))))

    def merge(x):
        return x.astype(F32).reshape(seq_len, x.shape[-1]).astype(BF16)

    def unit_major(x):
        x = x.astype(F32).reshape(seq_n, units, unit, x.shape[-1])
        return jnp.transpose(x, (1, 0, 2, 3)).reshape(seq_len, x.shape[-1]).astype(BF16)

    def one_head(h, carry):
        base = pl.multiple_of(h * 3 * HEAD_DIM, HEAD_DIM)
        q = unit_major(heads[:, :, pl.ds(base, HEAD_DIM)])
        key = merge(heads[:, :, pl.ds(pl.multiple_of(base + HEAD_DIM, HEAD_DIM), HEAD_DIM)])
        v = merge(heads[:, :, pl.ds(pl.multiple_of(base + 2 * HEAD_DIM, HEAD_DIM), HEAD_DIM)])
        sc = lax.dot_general(q, key, (((1,), (1,)), ((), ())), preferred_element_type=F32)
        sc = sc * HEAD_DIM ** (-0.5)
        e = jnp.exp(sc - jnp.max(sc, axis=-1, keepdims=True))
        w = (e / jnp.sum(e, axis=-1, keepdims=True)).astype(BF16)
        o = jnp.dot(w, v, preferred_element_type=F32).astype(BF16)
        att[:, pl.ds(pl.multiple_of(h * HEAD_DIM, HEAD_DIM), HEAD_DIM)] = o
        return carry

    tile = tile_of(width, 512)
    wide = tile_of(wcols, 512)
    state = {}
    kept_out = []
    batches = batches_of(n_c)

    def project(g):
        k0, k1 = groups[g][0] * HEAD_DIM, sum(groups[g]) * HEAD_DIM

        def step(t, carry):
            c0 = pl.ds(pl.multiple_of(t * tile, 128), tile)
            y = jnp.dot(att[:, k0:k1], wout_v[k0:k1, c0], preferred_element_type=F32)
            if g > 0:
                y = y + head_sum[:, c0]
            if g < len(groups) - 1:
                head_sum[:, c0] = y
            else:
                y = y.reshape(units, seq_n, unit, tile).astype(BF16)
                for u in range(units):
                    part[:, u, :, c0] = y[u]
            return carry

        lax.fori_loop(0, width // tile, step, 0)

    def reduce(c):
        u0, u1 = chunks[c]
        n = u1 - u0
        us = pl.ds(u0, n)
        if not line:
            state["rs", c] = [
                start(push(
                    part.at[lax.rem(s + k, seq_n), us], rs_in.at[s, us],
                    rs_s.at[c, k], rs_r.at[c, k], (d, lax.rem(s + k, seq_n)),
                ))
                for k in order
            ]
            return
        pair = push(
            part.at[pl.ds(lo, 2), us], rs_in.at[pl.ds(lo, 2), us], rs_s.at[c, 1], rs_r.at[c, 1], (d, beside)
        )
        ends_sent.append(pair)
        state["pair", c] = pair

        @pl.when(jnp.logical_not(middle))
        def _():
            pair.start()

        state["rs", c] = [
            start(push(part.at[beside, us], rs_in.at[beside, us], rs_s.at[c, 0], rs_r.at[c, 0], (d, beside)))
        ]

    def relay_sum(c):
        if not line:
            return
        u0, u1 = chunks[c]
        us = pl.ds(u0, u1 - u0)
        across = [
            push(fwd.at[z - lo, us], rs_x.at[us], x_s.at[c, i], x_r.at[c], (d, z))
            for i, z in enumerate((mirror, mirror_beside))
        ]
        middle_sent.extend(across)
        state["rs", c].append(across[0])

        @pl.when(middle)
        def _():
            state["pair", c].wait_recv()
            for i in range(2):
                for u in range(u0, u1):
                    fwd[i, u] = (part[lo + i, u].astype(F32) + rs_in[lo + i, u].astype(F32)).astype(BF16)
            for cp in across:
                cp.start()

    def update(c):
        u0, u1 = chunks[c]
        if c == 0:
            hid_copy.wait()
        for cp in state["rs", c]:
            cp.wait_recv()
        for u in range(u0, u1):
            kept = []
            squares = jnp.zeros((unit, piece), F32)
            for j in range(dom_n):
                c0 = slice(j * piece, (j + 1) * piece)
                total = part[s, u, :, c0].astype(F32)
                if line:
                    total = total + rs_in[s, u, :, c0].astype(F32) + rs_x[u, :, c0].astype(F32)
                else:
                    for k in range(1, seq_n):
                        total = total + rs_in[lax.rem(s + k, seq_n), u, :, c0].astype(F32)
                x = (hid_v[u, :, c0].astype(F32) + gate_ref[:, c0] * total).astype(BF16)
                pieces_h[j, u] = x
                x = x.astype(F32)
                squares = squares + x * x
                kept.append(x)
            inv = lax.rsqrt(jnp.sum(squares, axis=-1, keepdims=True) / width + 1e-06)
            for j in range(dom_n):
                c0 = slice(j * piece, (j + 1) * piece)
                pieces_n[j, u] = (kept[j] * inv * (1.0 + scale_ref[:, c0])).astype(BF16)
        state["n", c] = [
            start(push(
                pieces_n.at[lax.rem(d + k, dom_n), pl.ds(u0, u1 - u0)], arrived[c].at[d],
                n_s.at[c, k], n_r.at[c, k], (lax.rem(d + k, dom_n), s),
            ))
            for k in range(1, dom_n)
        ]
        arrived[c][d] = pieces_n[d, u0:u1]
        state.setdefault("h", []).extend(
            start(push(
                pieces_h.at[lax.rem(d + k, dom_n), pl.ds(u0, u1 - u0)], arrived_h.at[d, pl.ds(u0, u1 - u0)],
                h_s.at[c, k], h_r.at[c, k], (lax.rem(d + k, dom_n), s),
            ))
            for k in range(1, dom_n)
        )
        arrived_h[d, u0:u1] = pieces_h[d, u0:u1]

    def route(c):
        u0, u1 = chunks[c]
        for cp in state["n", c]:
            cp.wait_recv()
        for p in range(dom_n):
            z_all[p // 2 // cx, p // 2 % cx, p % 2, s, u0:u1] = arrived[c][anc_ref[p]]

        def block(z):
            return z_all.at[:, :, :, z, pl.ds(u0, u1 - u0)]

        def give(z, to, i):
            return push(block(z), block(z), z_s.at[c, i], z_r.at[c, i], (d, to))

        if not line:
            state["z", c] = [start(give(s, lax.rem(s + k, seq_n), k)) for k in order]
            return
        far = start(give(s, mirror, 1))
        state["z1", c] = [start(give(s, beside, 0)), far]
        if c >= n_c - DIRECT:
            state["onward", c] = None
            state["z", c] = [start(give(s, mirror_beside, 2))]
            hand(c, 0, s)
            return
        onward = [
            push(block(z), block(z), z_s.at[c, 2 + i], z_r.at[c, 2], (d, to))
            for i, (z, to) in enumerate(((beside, mirror), (mirror, beside)))
        ]
        middle_sent.extend(onward)
        state["onward", c] = onward
        state["z", c] = onward[:1]
        hand(c, 0, s)

    def relay_rows(c):
        if not line:
            return
        for i, (cp, z) in enumerate(zip(state["z1", c], (beside, mirror))):
            cp.wait_recv()
            if state["onward", c] is not None:
                after = state["onward", c][i]

                @pl.when(middle)
                def _(after=after):
                    after.start()

            hand(c, 1 + i, z)

    def route_hidden():
        for cp in state["h"]:
            cp.wait_recv()
        for p in range(dom_n):
            routed_h[p] = arrived_h[anc_ref[p]]
        state["b"] = [
            start(push(
                routed_h.at[lax.rem(d + k, dom_n)], landed.at[d],
                b_s.at[k], b_r.at[k], (lax.rem(d + k, dom_n), s),
            ))
            for k in range(1, dom_n)
        ]
        landed[d] = routed_h[d]

    def finish_hidden():
        for cp in state["b"]:
            cp.wait_recv()
        for j in range(dom_n):
            nh_v[:, :, j * piece:(j + 1) * piece] = landed[j]
        kept_out.append(keep(nh_v, nh_ref, loc_sem.at[0]))

    def hand(c, b, z):
        u0, u1 = chunks[c]
        us = pl.ds(u0, u1 - u0)
        zs = slice(None) if z is None else z
        copies = state.setdefault(("l", c), [])
        for q in range(cy):
            for kk in range(2):
                if q + kk:
                    r, k, i = lax.rem(row + q, cy), core + kk - 2 * kk * core, q * 2 + kk
                    copies.append(start(push(
                        z_all.at[r, :, k, zs, us], lhs_a.at[slot_a, :, zs, us],
                        la_s.at[c, b, i], la_r.at[c, b, i], dev(r, col, k),
                    )))
        for q in range(cx):
            for kk in range(2):
                if q + kk:
                    r, k, i = lax.rem(col + q, cx), core + kk - 2 * kk * core, q * 2 + kk
                    copies.append(start(push(
                        z_all.at[:, r, k, zs, us], lhs_b.at[slot_b, :, zs, us],
                        lb_s.at[c, b, i], lb_r.at[c, b, i], dev(row, r, k),
                    )))

    def hand_out(c):
        u0, u1 = chunks[c]
        us = pl.ds(u0, u1 - u0)
        for cp in state["z", c]:
            cp.wait_recv()
        if line:
            hand(c, 3, mirror_beside)
        else:
            hand(c, 0, None)
        state["oa", c] = keep(z_all.at[row, :, core, :, us], lhs_a.at[slot_a, :, :, us], own_sem.at[c, 0])
        state["ob", c] = keep(z_all.at[:, col, core, :, us], lhs_b.at[slot_b, :, :, us], own_sem.at[c, 1])

    def multiply(g):
        c0, c1 = batches[g]
        c = g
        u0, u1 = chunks[c0][0], chunks[c1 - 1][1]
        n = u1 - u0
        m = seq_n * n * unit
        if c == 0:
            own_a.wait()
            own_b.wait()
            for cp in mate_copies:
                cp.wait_recv()
        for i in range(c0, c1):
            state["oa", i].wait()
            state["ob", i].wait()
            for cp in state["l", i]:
                cp.wait_recv()
        halves = (
            (lhs_a, act_a, w_a, snd_a, rcv_a, oa_s, oa_r, col, cx),
            (lhs_b, act_b, w_b, snd_b, rcv_b, ob_s, ob_r, row, cy),
        )
        for lhs, act, w, snd, rcv, ss, rr, here, many in halves:
            for q in range(many):
                for j in range(lhs.shape[0]):
                    x = lhs[j, lax.rem(here + q, many), :, u0:u1].astype(F32)
                    act[q * m:(q + 1) * m, j * piece:(j + 1) * piece] = x.reshape(m, piece).astype(BF16)
        for t in range(wcols // wide):
            state["o", c, t] = []
            for half, (lhs, act, w, snd, rcv, ss, rr, here, many) in enumerate(halves):
                t0 = slice(t * wide, (t + 1) * wide)
                y = jnp.dot(act[:many * m, :], w[:, t0], preferred_element_type=F32)
                y = y.reshape(many, seq_n, n, unit, wide)
                acc[:, u0:u1, :, half * wcols + t * wide:half * wcols + (t + 1) * wide] = y[0]
                for q in range(1, many):
                    snd[q - 1, :, u0:u1, :, t0] = y[q].astype(BF16)
                    to = lax.rem(here + q, many)
                    block = (q - 1, slice(None), pl.ds(u0, n), slice(None), pl.ds(t * wide, wide))
                    state["o", c, t].append(start(push(
                        snd.at[block], rcv.at[block], ss.at[c, q, t], rr.at[c, q, t],
                        dev(row, to, core) if half == 0 else dev(to, col, core),
                    )))

    def finish(g):
        c = g
        u0, u1 = chunks[batches[g][0]][0], chunks[batches[g][1] - 1][1]
        for t in range(wcols // wide):
            for cp in state["o", c, t]:
                cp.wait_recv()
            for half, (rcv, many) in enumerate(((rcv_a, cx), (rcv_b, cy))):
                o0 = slice(half * wcols + t * wide, half * wcols + (t + 1) * wide)
                y = acc[:, u0:u1, :, o0]
                for q in range(1, many):
                    y = y + rcv[q - 1, :, u0:u1, :, t * wide:(t + 1) * wide].astype(F32)
                out_v[:, u0:u1, :, o0] = y.astype(BF16)

        kept_out.append(keep(out_v.at[:, pl.ds(u0, u1 - u0)], out_ref.at[:, pl.ds(u0, u1 - u0)], out_sem.at[g]))

    spread_weights()
    for g, (first, count) in enumerate(groups):
        own_heads[g].wait()
        for c in q_copies[g]:
            c.wait_recv()
        lax.fori_loop(first, first + count, one_head, 0)
        if g == 0:
            wout_copy.wait()
        project(g)
    for c in range(min(AHEAD, n_c)):
        reduce(c)
    def drain():
        for c in sent:
            c.wait_send()
        sent.clear()
        if line:
            @pl.when(middle)
            def _():
                for c in middle_sent:
                    c.wait_send()

            @pl.when(jnp.logical_not(middle))
            def _():
                for c in ends_sent:
                    c.wait_send()

    stages = (relay_sum, update, route, relay_rows, hand_out)
    last = {b[1] - 1: g for g, b in enumerate(batches)}
    for t in range(n_c + OFFSETS[-1]):
        if t + AHEAD < n_c:
            reduce(t + AHEAD)
        for off, stage in zip(OFFSETS, stages):
            c = t - off
            if 0 <= c < n_c:
                stage(c)
            if c == n_c - 1 and stage is route:
                route_hidden()
            if c == n_c - 1 and stage is hand_out:
                finish_hidden()
        if t - OFFSETS[5] in last:
            multiply(last[t - OFFSETS[5]])
        if last.get(t - OFFSETS[6], -1) == len(batches) - 1:
            drain()
        if t - OFFSETS[6] in last:
            finish(last[t - OFFSETS[6]])
        if t == FORWARD:
            forward_weights()
    for c in sent:
        c.wait_send()
    for c in kept_out:
        c.wait()


def body(dom_n, seq_n, hidden, qkv, w_out, gate, next_scale, ancestors, w_next):
    _, rows, width = hidden.shape
    unit = unit_of(rows)
    units = rows // unit
    chunks = chunks_of(units)
    n_c = len(chunks)
    cols = qkv.shape[2] // seq_n
    seq_len = rows * seq_n
    out_cols = w_next.shape[1]
    wcols = out_cols // 2
    att_cols = w_out.shape[0]
    cy, cx = grid_of(dom_n)
    piece = width // dom_n
    n_t = wcols // tile_of(wcols, 512)
    n_g = len(groups_of(cols // (3 * HEAD_DIM)))
    most = max(chunks[c1 - 1][1] - chunks[c0][0] for c0, c1 in batches_of(n_c)) * seq_n * unit
    sem = pltpu.SemaphoreType.DMA
    any_spec = pl.BlockSpec(memory_space=pl.ANY)
    vmem = pl.BlockSpec(memory_space=pltpu.VMEM)

    def buf(*shape, dtype=BF16):
        return pltpu.VMEM(shape, dtype)

    nh, out = pl.pallas_call(
        functools.partial(kernel, dom_n, seq_n, chunks),
        out_shape=(
            jax.ShapeDtypeStruct((units, unit, width), BF16),
            jax.ShapeDtypeStruct((seq_n, units, unit, out_cols), BF16),
        ),
        in_specs=[
            pl.BlockSpec(memory_space=pltpu.SMEM), any_spec, any_spec, any_spec, vmem, vmem, any_spec,
        ],
        out_specs=(any_spec, any_spec),
        scratch_shapes=[
            buf(seq_n, rows, cols),
            buf(att_cols, width),
            buf(units, unit, width),
            buf(seq_len, att_cols),
            buf(seq_n, units, unit, width),
            buf(seq_n, units, unit, width),
            buf(units, unit, width),
            buf(2, units, unit, width),
            buf(dom_n, units, unit, piece),
            buf(dom_n, units, unit, piece),
            *[buf(dom_n, u1 - u0, unit, piece) for u0, u1 in chunks],
            buf(dom_n, units, unit, piece),
            buf(dom_n, units, unit, piece),
            buf(dom_n, units, unit, piece),
            buf(cy, cx, 2, seq_n, units, unit, piece),
            buf(2 * cy, cx, seq_n, units, unit, piece),
            buf(2 * cx, cy, seq_n, units, unit, piece),
            buf(cx * most, 2 * cy * piece),
            buf(cy * most, 2 * cx * piece),
            buf(2 * cy * w_next.shape[0], wcols),
            buf(2 * cx * w_next.shape[0], wcols),
            buf(seq_n, units, unit, out_cols, dtype=F32),
            buf(max(cx - 1, 1), seq_n, units, unit, wcols),
            buf(max(cy - 1, 1), seq_n, units, unit, wcols),
            buf(max(cx - 1, 1), seq_n, units, unit, wcols),
            buf(max(cy - 1, 1), seq_n, units, unit, wcols),
            sem((4 + n_g,)),
            sem((n_g, seq_n)), sem((n_g, seq_n)),
            sem((n_c, seq_n)), sem((n_c, seq_n)),
            sem((n_c, 2)), sem((n_c,)),
            sem((n_c, dom_n)), sem((n_c, dom_n)),
            sem((n_c, seq_n)), sem((n_c, seq_n)),
            sem((n_c, 4, 2 * cy)), sem((n_c, 4, 2 * cy)),
            sem((n_c, 4, 2 * cx)), sem((n_c, 4, 2 * cx)),
            sem((n_c, cx, n_t)), sem((n_c, cx, n_t)),
            sem((n_c, cy, n_t)), sem((n_c, cy, n_t)),
            sem((n_c, dom_n)), sem((n_c, dom_n)),
            sem((dom_n,)), sem((dom_n,)),
            sem((cy,)), sem((cy,)),
            sem((cx,)), sem((cx,)),
            sem((cy,)), sem((cy,)),
            sem((cx,)), sem((cx,)),
            sem((n_c, 2)),
            sem((n_c,)),
            buf(units, unit, width),
            buf(seq_n, units, unit, out_cols),
            buf(seq_len, width, dtype=F32),
        ],
        compiler_params=pltpu.CompilerParams(
            collective_id=0, has_side_effects=True, vmem_limit_bytes=60 * 1024 * 1024
        ),
    )(
        ancestors, hidden.reshape(units, unit, width), qkv, w_out, gate[None], next_scale[None], w_next
    )
    nh, out = settle(nh, out)
    return nh.reshape(1, rows, width), out.reshape(1, seq_len, out_cols)


def settle_kernel(a_ref, b_ref, a_out, b_out, a_v, b_v, sem_in, sem_out):
    pairs = [(a_ref, a_v, a_out)] + [(b_ref.at[i], b_v.at[i], b_out.at[i]) for i in range(b_ref.shape[0])]
    reads = [pltpu.make_async_copy(x, v, sem_in.at[i]) for i, (x, v, _) in enumerate(pairs)]
    writes = [pltpu.make_async_copy(v, y, sem_out.at[i]) for i, (_, v, y) in enumerate(pairs)]
    for c in reads:
        c.start()
    for r, w in zip(reads, writes):
        r.wait()
        w.start()
    for c in writes:
        c.wait()


def settle(a, b):
    spec = pl.BlockSpec(memory_space=pl.ANY)
    sems = pltpu.SemaphoreType.DMA((1 + b.shape[0],))
    return pl.pallas_call(
        settle_kernel,
        out_shape=(jax.ShapeDtypeStruct(a.shape, a.dtype), jax.ShapeDtypeStruct(b.shape, b.dtype)),
        in_specs=[spec, spec],
        out_specs=(spec, spec),
        scratch_shapes=[pltpu.VMEM(a.shape, a.dtype), pltpu.VMEM(b.shape, b.dtype), sems, sems],
        compiler_params=pltpu.CompilerParams(vmem_limit_bytes=60 * 1024 * 1024),
    )(a, b)


def solution(mesh):
    in_specs = (
        P("dom", "seq", None),
        P("dom", "seq", None),
        P("seq", None),
        P(),
        P(),
        P(),
        P("dom", "seq"),
    )
    out_specs = (P("dom", "seq", None), P("dom", None, "seq"))
    return jax.shard_map(
        functools.partial(body, mesh.shape["dom"], mesh.shape["seq"]),
        mesh=mesh, in_specs=in_specs, out_specs=out_specs, check_vma=False,
    )
```
